256 devices in a mesh: section: 4 (over z_hi), ep: 64 (over y, x, z_lo, core).
Axes of the slice: x: 4, y: 4, z: 8 (z_hi: 4, z_lo: 2; z = z_hi * 2 + z_lo), core: 2. Of those that a mesh axis runs over, the one named last changes fastest.
Arguments:
- fresh_tokens: bfloat16 [1024, 3584], P('ep'), may hold values from -6 to 6
- sent_forward: bfloat16 [4, 1024, 3584], P('section', 'ep'), may hold values from -6 to 6
- sent_backward: bfloat16 [4, 1024, 3584], P('section', 'ep'), may hold values from -1.1953125 to 1.1953125
- turn_gradient: bfloat16 [1024, 3584], P('ep'), may hold values from -1.1953125 to 1.1953125
- saved_input: bfloat16 [4, 1024, 3584], P('section', 'ep'), may hold values from -6 to 6
- gain: bfloat16 [4, 3584], P('section'), may hold values from 0.5 to 1.5
- ids_front: int32 [4, 1024, 2], P('section', 'ep'), may hold values from 0 to 7, all different within a row; in each aligned block of 16 rows (0 to 15, 16 to 31, ..., all dimensions but the last counted through in order) at most 8 rows name the same one
- affinity_front: float32 [4, 1024, 2], P('section', 'ep'), may hold values from 0.1 to 1
- ids_back: int32 [4, 1024, 2], P('section', 'ep'), may hold values from 0 to 7, all different within a row; in each aligned block of 16 rows (0 to 15, 16 to 31, ..., all dimensions but the last counted through in order) at most 8 rows name the same one
- affinity_back: float32 [4, 1024, 2], P('section', 'ep'), may hold values from 0.1 to 1
- w_gate: bfloat16 [4, 3584, 8192], P('section', None, 'ep'), may hold values from -0.09375 to 0.09375
- w_up: bfloat16 [4, 3584, 8192], P('section', None, 'ep'), may hold values from -0.09375 to 0.09375
- w_down: bfloat16 [4, 8192, 3584], P('section', 'ep'), may hold values from -0.1875 to 0.1875
- mirror_gate: bfloat16 [4, 3584, 8192], P('section', None, 'ep'), may hold values from -6 to 6
- mirror_up: bfloat16 [4, 3584, 8192], P('section', None, 'ep'), may hold values from -6 to 6
- mirror_down: bfloat16 [4, 8192, 3584], P('section', 'ep'), may hold values from -6 to 6
Outputs:
- forward_out: bfloat16 [4, 1024, 3584], P('section', 'ep')
- grad_input: bfloat16 [4, 1024, 3584], P('section', 'ep')
- grad_gate: bfloat16 [4, 3584, 8192], P('section', None, 'ep')
- grad_up: bfloat16 [4, 3584, 8192], P('section', None, 'ep')
- grad_down: bfloat16 [4, 8192, 3584], P('section', 'ep')
The draws below stay inside these ranges and needn't reach their ends.
Inputs may be any that keep to these rules, and one draw needn't show every extreme that they name: `ids_front`: each row names 2 different experts. In each aligned block of 16 rows (the rows of one device) no expert is named by more than 8 rows, a bound that some block reaches. `ids_back`: each row names 2 different experts. In each aligned block of 16 rows (the rows of one device) no expert is named by more than 8 rows, a bound that some block reaches.
All inputs are finite; a program needn't handle non-finite values.
Results may differ from the reference program's by a relative error of at most 0.0068.
Values may be sent and summed in bfloat16 or wider, within the bound.
A program may use at most 128 MiB of HBM per device.

```python
import math
import jax
import jax.numpy as jnp
import numpy as np
from jax import lax

D = 3584
H = 1024
EXPERTS = 8
TOP = 2
TOK = 16
GROUP = 8
SLICE = 128
CAP = 8
TOKENS = 1024
UNITS = 8192
N_SECTION = 4
N_EP = 64


def levels(stream_key, dims, pieces, smallest, largest):
    factor_of, own = 1.0, jax.random.fold_in(stream_key, 6)
    for dim, blocks in pieces:
        heights = jnp.exp(jax.random.uniform(jax.random.fold_in(own, dim), (blocks,), jnp.float32, smallest / len(pieces), largest / len(pieces)))
        factor_of = factor_of * jnp.repeat(heights, dims[dim] // blocks).reshape([-1 if axis == dim else 1 for axis in range(len(dims))])
    return factor_of


def shared_out(key, own, number, rows, number_of, top, bound, skew):
    ranking = jax.random.permutation(key, number_of)
    crowded, ordinary = load_shares(number_of, rows * top, bound, skew, True), load_shares(number_of, rows * top, bound, skew, False)
    places = jnp.arange(number_of)

    def named(lengths, rotation):
        used = int((lengths > 0).sum())
        fixed = max(1, used // 4)
        shifted = fixed + (places - fixed + rotation * (used - fixed)) % max(1, number_of - fixed)
        return jnp.zeros((number_of,), jnp.int32).at[ranking[jnp.where(places < fixed, places, shifted)]].set(jnp.asarray(lengths, jnp.int32))

    lengths = jnp.where(number % 4 == 0, named(crowded, number // 4), named(ordinary, number - number // 4 - 1))
    mixed = jax.random.permutation(jax.random.fold_in(own, 3), number_of)
    source_of, sink = mixed[0:number_of // 2 * 2:2], mixed[1:number_of // 2 * 2:2]
    room = jnp.minimum(lengths[source_of] - 1, bound - lengths[sink]) // 2
    room = jnp.where((source_of == ranking[0]) | (sink == ranking[0]) | (lengths[sink] == 0), 0, jnp.maximum(room, 0))
    shifted = jax.random.randint(jax.random.fold_in(own, 4), (number_of // 2,), 0, 1 << 20) % (room + 1)
    lengths = lengths.at[source_of].add(-shifted).at[sink].add(shifted)
    items = jnp.searchsorted(jnp.cumsum(lengths), jnp.arange(rows * top), side="right").astype(jnp.int32)
    grid = items.reshape(top, rows).T
    grid = grid[jax.random.permutation(jax.random.fold_in(own, 1), rows)]
    rotation = jax.random.randint(jax.random.fold_in(own, 2), (rows, 1), 0, top)
    return jnp.take_along_axis(grid, (jnp.arange(top)[None, :] + rotation) % top, axis=1)


def load_shares(number_of, total, most, lean, full):
    loads = [(1 << 20) // math.isqrt(rank ** lean) + 1 for rank in range(1, number_of + 1)]
    largest = most if full else min(most, max(-(-total // number_of), total * loads[0] // sum(loads)))
    least = 1 if total - largest >= number_of - 1 else 0
    given, spare = [largest] + [least] * (number_of - 1), total - largest - least * (number_of - 1)
    while spare > 0:
        free = [i for i in range(1, number_of) if given[i] < largest] or [i for i in range(1, number_of) if given[i] < most]
        mass, budget = sum([loads[i] for i in free]), spare
        for i in free:
            extra = min(most - given[i], max(1, budget * loads[i] // mass), spare)
            given[i] = given[i] + extra
            spare = spare - extra
    return np.array(given)


def normal_values(stream_key, shape, width, bound, shards=(), kind=jnp.bfloat16):
    level = levels(stream_key, shape, shards, -0.22, 0.18) if shards else 1.0
    drawn = jax.random.normal(stream_key, shape, jnp.float32) * width * level
    return jnp.minimum(jnp.maximum(drawn, -bound), bound).astype(kind)


def setup_inputs(seed: int = 0) -> dict:
    streams_of = jax.random.split(jax.random.key(seed), 17)
    fresh_tokens = normal_values(streams_of[0], (TOKENS, D), 1.0, 6.0, ((0, 64),))
    sent_forward = normal_values(streams_of[1], (N_SECTION, TOKENS, D), 1.0, 6.0, ((0, 4), (1, 64)))
    sent_backward = normal_values(streams_of[2], (N_SECTION, TOKENS, D), 0.2, 1.1953125, ((0, 4), (1, 64)))
    turn_gradient = normal_values(streams_of[3], (TOKENS, D), 0.2, 1.1953125, ((0, 64),))
    saved_input = normal_values(streams_of[4], (N_SECTION, TOKENS, D), 1.0, 6.0, ((0, 4), (1, 64)))
    gain = jnp.clip(1.0 + 0.1 * jax.random.normal(streams_of[5], (N_SECTION, D), jnp.float32), 0.5, 1.5).astype(jnp.bfloat16)
    ids_front_keys = jax.random.split(jax.random.fold_in(streams_of[6], 1), N_SECTION * TOKENS // TOK)
    ids_front_turns = jax.random.permutation(jax.random.fold_in(streams_of[6], 3), N_SECTION * TOKENS // TOK)
    ids_front = jax.vmap(lambda own, number: shared_out(jax.random.fold_in(streams_of[6], 2), own, number, TOK, EXPERTS, TOP, CAP, 2))(ids_front_keys, ids_front_turns).reshape((N_SECTION, TOKENS, TOP))
    affinity_front = jnp.clip(jnp.exp(math.log(1.0) - 2.3025851 * jax.random.uniform(streams_of[7], (N_SECTION, TOKENS, TOP), jnp.float32) ** levels(streams_of[7], (N_SECTION, TOKENS, TOP), ((0, 4), (1, 64)), -0.2, 0.2)), 0.1, 1.0)
    ids_back_keys = jax.random.split(jax.random.fold_in(streams_of[8], 1), N_SECTION * TOKENS // TOK)
    ids_back_turns = jax.random.permutation(jax.random.fold_in(streams_of[8], 3), N_SECTION * TOKENS // TOK)
    ids_back = jax.vmap(lambda own, number: shared_out(jax.random.fold_in(streams_of[8], 2), own, number, TOK, EXPERTS, TOP, CAP, 2))(ids_back_keys, ids_back_turns).reshape((N_SECTION, TOKENS, TOP))
    affinity_back = jnp.clip(jnp.exp(math.log(1.0) - 2.3025851 * jax.random.uniform(streams_of[9], (N_SECTION, TOKENS, TOP), jnp.float32) ** levels(streams_of[9], (N_SECTION, TOKENS, TOP), ((0, 4), (1, 64)), -0.2, 0.2)), 0.1, 1.0)
    w_gate = normal_values(streams_of[10], (N_SECTION, D, UNITS), D ** -0.5, 0.09375, ((0, 4), (2, 64)))
    w_up = normal_values(streams_of[11], (N_SECTION, D, UNITS), D ** -0.5, 0.09375, ((0, 4), (2, 64)))
    w_down = normal_values(streams_of[12], (N_SECTION, UNITS, D), H ** -0.5, 0.1875, ((0, 4), (1, 64)))
    mirror_gate = normal_values(streams_of[13], (N_SECTION, D, UNITS), 1.0, 6.0, ((0, 4), (2, 64)))
    mirror_up = normal_values(streams_of[14], (N_SECTION, D, UNITS), 1.0, 6.0, ((0, 4), (2, 64)))
    mirror_down = normal_values(streams_of[15], (N_SECTION, UNITS, D), 1.0, 6.0, ((0, 4), (1, 64)))
    return {"fresh_tokens": fresh_tokens, "sent_forward": sent_forward, "sent_backward": sent_backward, "turn_gradient": turn_gradient, "saved_input": saved_input, "gain": gain, "ids_front": ids_front, "affinity_front": affinity_front, "ids_back": ids_back, "affinity_back": affinity_back, "w_gate": w_gate, "w_up": w_up, "w_down": w_down, "mirror_gate": mirror_gate, "mirror_up": mirror_up, "mirror_down": mirror_down}


highest = lax.Precision.HIGHEST

def silu_of(pre_act):
    return pre_act * jax.nn.sigmoid(pre_act)

def rounded(values):
    return lax.optimization_barrier(values.astype(jnp.bfloat16)).astype(jnp.float32)

def norm_rows(inputs, gain):
    values = inputs.astype(jnp.float32)
    inverse = lax.rsqrt(lax.optimization_barrier(jnp.mean(values * values, axis=-1, keepdims=True)) + 1e-06)
    normed = (values * inverse * gain.astype(jnp.float32)).astype(jnp.bfloat16)
    return (values, inverse, normed)

def slot_tables(route_ids, affinity, capacity):
    flat_ids = route_ids.reshape(-1)
    onehot = (flat_ids[:, None] == jnp.arange(EXPERTS, dtype=jnp.int32)[None, :]).astype(jnp.int32)
    earlier = jnp.cumsum(onehot, axis=0) - onehot
    position = lax.optimization_barrier(jnp.sum(earlier * onehot, axis=1))
    target = (flat_ids * capacity + position).reshape(route_ids.shape)
    columns = jnp.arange(EXPERTS * capacity, dtype=jnp.int32)
    matches = (target[:, :, None] == columns[None, None, :]).astype(jnp.float32)
    shares = affinity / lax.optimization_barrier(jnp.sum(affinity, axis=1, keepdims=True))
    return (lax.optimization_barrier(jnp.sum(matches, axis=1)), lax.optimization_barrier(jnp.sum(matches * shares[:, :, None], axis=1)))

def route_tables(route_ids, affinity):

    def one_block(ids_block, aff_block):
        return slot_tables(ids_block, aff_block, CAP)
    return jax.vmap(one_block)(route_ids.reshape(N_EP, TOK, TOP), affinity.reshape(N_EP, TOK, TOP))

def expert_forward(token_rows, gate_cols, up_cols, down_rows):
    gate_pre = jnp.dot(token_rows, gate_cols, preferred_element_type=jnp.float32)
    up_pre = jnp.dot(token_rows, up_cols, preferred_element_type=jnp.float32)
    hidden = (silu_of(gate_pre) * up_pre).astype(jnp.bfloat16)
    total = jnp.zeros((token_rows.shape[0], D), jnp.float32)
    for piece in range(GROUP):
        part_cols = slice(piece * SLICE, (piece + 1) * SLICE)
        total = total + rounded(jnp.dot(hidden[:, part_cols], down_rows[part_cols], preferred_element_type=jnp.float32))
    return total

def expert_backward(token_rows, grad_rows, gate_cols, up_cols, down_rows):
    gate_pre = jnp.dot(token_rows, gate_cols, preferred_element_type=jnp.float32)
    up_pre = jnp.dot(token_rows, up_cols, preferred_element_type=jnp.float32)
    gate_sig = jax.nn.sigmoid(gate_pre)
    active = gate_pre * gate_sig
    hidden = (active * up_pre).astype(jnp.bfloat16)
    grad_hidden = jnp.dot(grad_rows, down_rows.T, preferred_element_type=jnp.float32)
    grad_down = jnp.dot(hidden.T, grad_rows, preferred_element_type=jnp.float32)
    grad_gate_pre = (grad_hidden * up_pre * gate_sig * (1.0 + gate_pre * (1.0 - gate_sig))).astype(jnp.bfloat16)
    grad_up_pre = (grad_hidden * active).astype(jnp.bfloat16)
    grad_gate = jnp.dot(token_rows.T, grad_gate_pre, preferred_element_type=jnp.float32)
    grad_up = jnp.dot(token_rows.T, grad_up_pre, preferred_element_type=jnp.float32)
    total = jnp.zeros((token_rows.shape[0], D), jnp.float32)
    for piece in range(GROUP):
        part_cols = slice(piece * SLICE, (piece + 1) * SLICE)
        term = jnp.dot(grad_gate_pre[:, part_cols], gate_cols[:, part_cols].T, preferred_element_type=jnp.float32)
        term = term + jnp.dot(grad_up_pre[:, part_cols], up_cols[:, part_cols].T, preferred_element_type=jnp.float32)
        total = total + rounded(term)
    return (grad_gate, grad_up, grad_down, total)

def pack_rows(member, normed):
    packed = jnp.einsum('btm,btd->bmd', member, normed.astype(jnp.float32))
    return packed.astype(jnp.bfloat16).reshape(N_EP, EXPERTS, CAP, D)

def forward_section(inputs, gain, route_ids, affinity, w_gate, w_up, w_down):
    values, inverse, normed = norm_rows(inputs.reshape(N_EP, TOK, D), gain)
    member, weighted = route_tables(route_ids, affinity)
    packed = pack_rows(member, normed)
    outputs = []
    for expert in range(EXPERTS):
        cols = slice(expert * H, (expert + 1) * H)
        token_rows = packed[:, expert].reshape(N_EP * CAP, D)
        outputs.append(expert_forward(token_rows, w_gate[:, cols], w_up[:, cols], w_down[cols]).reshape(N_EP, CAP, D))
    totals = jnp.stack(outputs, axis=1).reshape(N_EP, EXPERTS * CAP, D)
    mixed = values + jnp.einsum('btm,bmd->btd', weighted, totals, precision=highest)
    return mixed.astype(jnp.bfloat16).reshape(TOKENS, D)

def backward_section(saved, cotangent, gain, route_ids, affinity, w_gate, w_up, w_down, mirror_gate, mirror_up, mirror_down):
    values, inverse, normed = norm_rows(saved.reshape(N_EP, TOK, D), gain)
    member, weighted = route_tables(route_ids, affinity)
    upstream = cotangent.reshape(N_EP, TOK, D).astype(jnp.float32)
    packed = pack_rows(member, normed)
    grad_packed = jnp.einsum('btm,btd->bmd', weighted, upstream, precision=highest)
    grad_packed = grad_packed.astype(jnp.bfloat16).reshape(N_EP, EXPERTS, CAP, D)
    gate_list, up_list, down_list, slot_list = ([], [], [], [])
    for expert in range(EXPERTS):
        cols = slice(expert * H, (expert + 1) * H)
        token_rows = packed[:, expert].reshape(N_EP * CAP, D)
        grad_rows = grad_packed[:, expert].reshape(N_EP * CAP, D)
        g_gate, g_up, g_down, total = expert_backward(token_rows, grad_rows, w_gate[:, cols], w_up[:, cols], w_down[cols])
        gate_list.append(g_gate)
        up_list.append(g_up)
        down_list.append(g_down)
        slot_list.append(total.reshape(N_EP, CAP, D))
    grad_gate = (mirror_gate.astype(jnp.float32) + jnp.concatenate(gate_list, axis=1)).astype(jnp.bfloat16)
    grad_up = (mirror_up.astype(jnp.float32) + jnp.concatenate(up_list, axis=1)).astype(jnp.bfloat16)
    grad_down = (mirror_down.astype(jnp.float32) + jnp.concatenate(down_list, axis=0)).astype(jnp.bfloat16)
    totals = jnp.stack(slot_list, axis=1).reshape(N_EP, EXPERTS * CAP, D)
    grad_normed = jnp.einsum('btm,bmd->btd', member, totals, precision=highest)
    scaled = grad_normed * gain.astype(jnp.float32)
    cubed = inverse * inverse * inverse
    grad_inputs = upstream + inverse * scaled - cubed * values * lax.optimization_barrier(jnp.mean(scaled * values, axis=-1, keepdims=True))
    return (grad_inputs.astype(jnp.bfloat16).reshape(TOKENS, D), grad_gate, grad_up, grad_down)

def reference(fresh_tokens, sent_forward, sent_backward, turn_gradient, saved_input, gain, ids_front, affinity_front, ids_back, affinity_back, w_gate, w_up, w_down, mirror_gate, mirror_up, mirror_down):
    forward_list, input_list, gate_list, up_list, down_list = ([], [], [], [], [])
    for section_id in range(N_SECTION):
        front_in = fresh_tokens if section_id == 0 else sent_forward[section_id - 1]
        upstream_in = turn_gradient if section_id == N_SECTION - 1 else sent_backward[section_id + 1]
        forward_list.append(forward_section(front_in, gain[section_id], ids_front[section_id], affinity_front[section_id], w_gate[section_id], w_up[section_id], w_down[section_id]))
        grad_inputs, grad_gate, grad_up, grad_down = backward_section(saved_input[section_id], upstream_in, gain[section_id], ids_back[section_id], affinity_back[section_id], w_gate[section_id], w_up[section_id], w_down[section_id], mirror_gate[section_id], mirror_up[section_id], mirror_down[section_id])
        input_list.append(grad_inputs)
        gate_list.append(grad_gate)
        up_list.append(grad_up)
        down_list.append(grad_down)
    return (jnp.stack(forward_list), jnp.stack(input_list), jnp.stack(gate_list), jnp.stack(up_list), jnp.stack(down_list))
```

```python
import functools
import jax
import jax.numpy as jnp
from jax import lax
from jax.experimental import pallas as pl
from jax.experimental.pallas import tpu as pltpu
from jax.sharding import PartitionSpec as P

BF = jnp.bfloat16
F32 = jnp.float32
MESH = pl.DeviceIdType.MESH
D = 3584
W = D // 2
TOK = 16
HID = 128
EXPERTS = 8
ROWS = 256
ROWS_B, GRADS, FRONT = 0, 1, 2
N_AG = 17
N_RS = 14


def kernel(
    fresh, sent_f, sent_b, turn, saved, gain, ids_f, aff_f, ids_b, aff_b,
    w_gate, w_up, w_down, m_gate, m_up, m_down,
    out_f, out_b, o_gate, o_up, o_down,
    g0, g1, pb, core_in, big_in, small_in, last_in, wgu, wd, mg, mu, md,
    dgu_t, hid_t, came_f, came_b,
    ag_send, ag_recv, rs_send, rs_recv, sec_send, sec_recv, load_sem, save_sem,
):
    sec = lax.axis_index("section")
    ep = lax.axis_index("ep")
    core = lax.rem(ep, 2)
    z = lax.rem(ep // 2, 2)
    x = lax.rem(ep // 4, 4)
    y = ep // 16
    expert = ep // 8

    def at(yy, xx, zz, cc):
        return (sec, ((yy * 4 + xx) * 2 + zz) * 2 + cc)

    def turn4(v, by):
        return lax.rem(v + by, 4)

    dev_z = at(y, x, 1 - z, core)
    dev_c = at(y, x, z, 1 - core)
    dev_y = (at(turn4(y, 1), x, z, core), at(turn4(y, 3), x, z, core))
    dev_x = (at(y, turn4(x, 1), z, core), at(y, turn4(x, 3), z, core))
    dev_s = ((turn4(sec, 1), ep), (turn4(sec, 3), ep))

    loads = [
        pltpu.make_async_copy(w_gate, wgu.at[:, pl.ds(0, HID)], load_sem.at[0]),
        pltpu.make_async_copy(w_up, wgu.at[:, pl.ds(HID, HID)], load_sem.at[1]),
        pltpu.make_async_copy(w_down, wd, load_sem.at[2]),
        pltpu.make_async_copy(m_gate, mg, load_sem.at[3]),
        pltpu.make_async_copy(m_up, mu, load_sem.at[4]),
        pltpu.make_async_copy(m_down, md, load_sem.at[5]),
    ]

    def remote(src, dst, send, recv, dev):
        return pltpu.make_async_remote_copy(
            src_ref=src, dst_ref=dst, send_sem=send, recv_sem=recv,
            device_id=dev, device_id_type=MESH,
        )

    pending = {0: [], 1: [], 2: []}

    def slot(u, s, cc, yy, xx):
        ref = (g0, g1)[s]
        if s == 0 and u == ROWS_B:
            return ref.at[u, cc, yy, xx, :, :, pl.ds(0, W)]
        return ref.at[u, cc, yy, xx]

    def ag(u, s):
        base = (u * 2 + s) * N_AG

        def put(k, ref, dev):
            copy = remote(ref, ref, ag_send.at[base + k], ag_recv.at[base + k], dev)
            copy.start()
            pending[u].append(copy)

        def got(k, ref):
            remote(ref, ref, ag_send.at[base + k], ag_recv.at[base + k], dev_c).wait_recv()

        put(0, slot(u, s, core, y, x).at[z], dev_z)
        yield
        got(0, slot(u, s, core, y, x).at[1 - z])

        def ring(k, blk, me, dev):
            left, right, far = turn4(me, 3), turn4(me, 1), turn4(me, 2)
            put(k, blk(me, 0), dev[0])
            put(k + 2, blk(me, 1), dev[1])
            put(k + 1, blk(me, 1), dev[0])
            put(k + 3, blk(me, 0), dev[1])
            yield
            got(k, blk(left, 0))
            put(k + 4, blk(left, 0), dev[0])
            got(k + 2, blk(right, 1))
            put(k + 5, blk(right, 1), dev[1])
            yield
            got(k + 1, blk(left, 1))
            got(k + 3, blk(right, 0))
            yield 1
            got(k + 4, blk(far, 0))
            got(k + 5, blk(far, 1))

        if s == 0:
            yield from ring(1, lambda i, h: slot(u, s, core, y, i).at[h], x, dev_x)
            whole = lambda i: slot(u, s, core, i, slice(None))
            half = lambda i, h: slot(u, s, core, i, pl.ds(2 * h, 2))
            me, dev = y, dev_y
        else:
            yield from ring(1, lambda i, h: slot(u, s, core, i, x).at[h], y, dev_y)
            whole = lambda i: slot(u, s, core, slice(None), i)
            half = lambda i, h: slot(u, s, core, pl.ds(2 * h, 2), i)
            me, dev = x, dev_x
        gen = ring(7, half, me, dev)
        next(gen)
        put(13, whole(me), dev_c)
        yield
        next(gen)
        yield
        next(gen)
        put(14, whole(turn4(me, 3)), dev_c)
        put(15, whole(turn4(me, 1)), dev_c)
        yield
        for _ in gen:
            pass
        put(16, whole(turn4(me, 2)), dev_c)
        yield
        for k, by in ((13, 0), (14, 3), (15, 1), (16, 2)):
            i = turn4(me, by)
            if s == 0:
                got(k, slot(u, s, 1 - core, i, slice(None)))
            else:
                got(k, slot(u, s, 1 - core, slice(None), i))

    done = []

    def part(u, s, cc, yy, xx):
        if u == 0:
            return pb.at[s, cc, yy, xx]
        if s == 0:
            return g0.at[FRONT, cc, yy, xx, :, :, pl.ds(0, W)]
        return g1.at[FRONT, cc, yy, xx]

    def add_into(dst, srcs, count):
        @pl.loop(0, count)
        def _(i):
            total = dst[i].astype(F32)
            for src in srcs:
                total = total + src[i].astype(F32)
            dst[i] = total.astype(BF)

    def rs(u, s):
        q = u * 2 + s
        base = q * N_RS

        def put(k, src, dst, dev):
            copy = remote(src, dst, rs_send.at[base + k], rs_recv.at[base + k], dev)
            copy.start()
            done.append(copy)

        def got(k, ref):
            remote(ref, ref, rs_send.at[base + k], rs_recv.at[base + k], dev_c).wait_recv()

        every = slice(None)
        put(0, part(u, s, 1 - core, every, every), core_in.at[q], dev_c)
        yield
        got(0, core_in.at[q])

        @pl.loop(0, 4)
        def _(yy):
            for xx in range(4):
                mine = part(u, s, core, yy, xx)
                mine[...] = (
                    mine[...].astype(F32) + core_in[q, yy, xx].astype(F32)
                ).astype(BF)

        def ring(k, blk, buf, me, dev, add):
            left, right, far = turn4(me, 3), turn4(me, 1), turn4(me, 2)
            put(k, blk(far, 0), buf(0, 0), dev[0])
            put(k + 1, blk(far, 1), buf(1, 0), dev[1])
            put(k + 2, blk(right, 1), buf(0, 2), dev[0])
            put(k + 3, blk(left, 0), buf(1, 1), dev[1])
            yield
            got(k, buf(0, 0))
            add(blk(right, 0), [buf(0, 0)])
            put(k + 4, blk(right, 0), buf(0, 1), dev[0])
            got(k + 1, buf(1, 0))
            add(blk(left, 1), [buf(1, 0)])
            put(k + 5, blk(left, 1), buf(1, 2), dev[1])
            yield
            got(k + 2, buf(0, 2))
            got(k + 3, buf(1, 1))
            yield
            got(k + 4, buf(0, 1))
            got(k + 5, buf(1, 2))
            add(blk(me, 0), [buf(0, 1), buf(1, 1)])
            add(blk(me, 1), [buf(0, 2), buf(1, 2)])

        def add_big(dst, srcs):
            @pl.loop(0, 2)
            def _(i):
                for j in range(2):
                    total = dst[i, j].astype(F32)
                    for src in srcs:
                        total = total + src[i, j].astype(F32)
                    dst[i, j] = total.astype(BF)

        def add_small(dst, srcs):
            total = dst[...].astype(F32)
            for src in srcs:
                total = total + src[...].astype(F32)
            dst[...] = total.astype(BF)

        big = lambda d, j: big_in.at[q, d, j]
        small = lambda d, j: small_in.at[q, d, j]
        if s == 0:
            yield from ring(1, lambda i, h: part(u, s, core, i, pl.ds(2 * h, 2)), big, y, dev_y, add_big)
            yield from ring(7, lambda i, h: part(u, s, core, y, i).at[h], small, x, dev_x, add_small)
        else:
            yield from ring(1, lambda i, h: part(u, s, core, pl.ds(2 * h, 2), i), big, x, dev_x, add_big)
            yield from ring(7, lambda i, h: part(u, s, core, i, x).at[h], small, y, dev_y, add_small)
        put(13, part(u, s, core, y, x).at[1 - z], last_in.at[q], dev_z)
        yield
        got(13, last_in.at[q])

    def total_of(u):
        halves = [
            part(u, s, core, y, x)[z].astype(F32) + last_in[u * 2 + s].astype(F32)
            for s in range(2)
        ]
        return jnp.concatenate(halves, axis=1)

    def rinv_of(v):
        return lax.rsqrt(jnp.mean(v * v, axis=-1, keepdims=True) + 1e-6)

    def place(u, value, weights=None):
        g0[u, core, y, x, z, :, pl.ds(0, W)] = value[:, :W]
        g1[u, core, y, x, z] = value[:, W:]
        if weights is not None:
            g0[u, core, y, x, z, :, pl.ds(W, 128)] = weights

    def norm(ref):
        v = ref.astype(F32)
        return (v * rinv_of(v) * gain[...].astype(F32)).astype(BF)

    def weights_of(ids, aff):
        share = aff[...] / jnp.sum(aff[...], axis=1, keepdims=True)
        lane = lax.broadcasted_iota(jnp.int32, (TOK, 128), 1)
        named = ids[...]
        out = jnp.zeros((TOK, 128), F32)
        for k in range(2):
            one = share[:, k : k + 1]
            high = one.astype(BF).astype(F32)
            out = out + jnp.where(lane == named[:, k : k + 1], high, 0.0)
            out = out + jnp.where(lane == named[:, k : k + 1] + EXPERTS, one - high, 0.0)
        return out.astype(BF)

    def chunk_at(i):
        return lax.rem(i // 2 + 1 - core, 2), (i % 2) * 2

    def rows_of(u, i):
        cc, yy = chunk_at(i)
        a = g0[u, cc, pl.ds(yy, 2), :, :, :, pl.ds(0, W)].reshape(ROWS, W)
        b = g1[u, cc, pl.ds(yy, 2)].reshape(ROWS, W)
        return a, b

    def share_of(u, i):
        cc, yy = chunk_at(i)
        aux = g0[u, cc, pl.ds(yy, 2), :, :, :, pl.ds(W, 128)].reshape(ROWS, 128).astype(F32)
        lane = lax.broadcasted_iota(jnp.int32, (ROWS, 128), 1)
        mine = (lane == expert) | (lane == expert + EXPERTS)
        return jnp.sum(jnp.where(mine, aux, 0.0), axis=1, keepdims=True)

    def dot(a, b):
        return jnp.dot(a, b, preferred_element_type=F32)

    def dot_t(a, b):
        return lax.dot_general(a, b, (((1,), (1,)), ((), ())), preferred_element_type=F32)

    def pre_acts(u, i):
        a, b = rows_of(u, i)
        gu = dot(a, wgu[pl.ds(0, W)]) + dot(b, wgu[pl.ds(W, W)])
        return gu[:, :HID], gu[:, HID:]

    TILE = 256

    def front_chunk(i):
        cc, yy = chunk_at(i)
        gate, up = pre_acts(FRONT, i)
        hidden = (gate * jax.nn.sigmoid(gate) * up * share_of(FRONT, i)).astype(BF)
        for s in range(2):
            @pl.loop(0, W // TILE)
            def _(n):
                lo = pl.multiple_of(n * TILE, TILE)
                res = dot(hidden, wd[:, pl.ds(s * W + lo, TILE)])
                (g0, g1)[s][FRONT, cc, pl.ds(yy, 2), :, :, :, pl.ds(lo, TILE)] = (
                    res.astype(BF).reshape(2, 4, 2, TOK, TILE)
                )

    def back_chunk(i):
        cc, yy = chunk_at(i)
        gate, up = pre_acts(ROWS_B, i)
        a, b = rows_of(GRADS, i)
        share = share_of(GRADS, i)
        sig = jax.nn.sigmoid(gate)
        active = gate * sig
        grad_hidden = (dot_t(a, wd[:, pl.ds(0, W)]) + dot_t(b, wd[:, pl.ds(W, W)])) * share
        dgate = grad_hidden * up * sig * (1.0 + gate * (1.0 - sig))
        dup = grad_hidden * active
        scaled = active * up * share
        lo = pl.multiple_of((cc * 2 + i % 2) * ROWS, ROWS)
        dgu_t[pl.ds(0, HID), pl.ds(lo, ROWS)] = dgate.T.astype(BF)
        dgu_t[pl.ds(HID, HID), pl.ds(lo, ROWS)] = dup.T.astype(BF)
        hid_t[:, pl.ds(lo, ROWS)] = scaled.T.astype(BF)
        both = jnp.concatenate([dgate, dup], axis=1).astype(BF)
        for s in range(2):
            @pl.loop(0, W // TILE)
            def _(n):
                lo = pl.multiple_of(n * TILE, TILE)
                res = dot_t(both, wgu[pl.ds(s * W + lo, TILE)])
                pb[s, cc, pl.ds(yy, 2), :, :, :, pl.ds(lo, TILE)] = (
                    res.astype(BF).reshape(2, 4, 2, TOK, TILE)
                )

    def grad_tiles(s, first, last):
        @pl.loop(first, last)
        def _(n):
            lo = pl.multiple_of(n * TILE, TILE)
            g = (g0, g1)[s]
            rows = g[ROWS_B, :, :, :, :, :, pl.ds(lo, TILE)].reshape(1024, TILE)
            here = pl.ds(s * W + lo, TILE)
            res = dot(dgu_t[...], rows)
            mg[here] = (mg[here].astype(F32) + res[:HID].T).astype(BF)
            mu[here] = (mu[here].astype(F32) + res[HID:].T).astype(BF)
            cot = g[GRADS, :, :, :, :, :, pl.ds(lo, TILE)].reshape(1024, TILE)
            md[:, here] = (md[:, here].astype(F32) + dot(hid_t[...], cot)).astype(BF)

    def step(*gens):
        for g in gens:
            next(g, None)

    def finish(*gens):
        for g in gens:
            for _ in g:
                pass

    barrier = pltpu.get_barrier_semaphore()
    for dev in (dev_z, dev_c, *dev_y, *dev_x, *dev_s):
        pl.semaphore_signal(barrier, inc=1, device_id=dev, device_id_type=MESH)
    pl.semaphore_wait(barrier, 8)

    sec_copies = [
        remote(sent_b, came_b, sec_send.at[0], sec_recv.at[0], dev_s[1]),
        remote(sent_f, came_f, sec_send.at[1], sec_recv.at[1], dev_s[0]),
    ]
    for copy in sec_copies:
        copy.start()
    for copy in loads:
        copy.start()
    place(ROWS_B, norm(saved[...]))
    b0, b1 = ag(ROWS_B, 0), ag(ROWS_B, 1)
    step(b0, b1)
    sec_copies[0].wait_recv()
    upstream = jnp.where(sec == 3, turn[...], came_b[...])
    came_b[...] = upstream
    place(GRADS, upstream, weights_of(ids_b, aff_b))
    step(b0, b1)
    c0, c1 = ag(GRADS, 0), ag(GRADS, 1)
    step(b0, b1)
    step(b0, b1)
    step(b0, b1)
    step(c0, c1)
    sec_copies[1].wait_recv()
    front = jnp.where(sec == 0, fresh[...], came_f[...])
    came_f[...] = front
    place(FRONT, norm(front), weights_of(ids_f, aff_f))
    f0, f1 = ag(FRONT, 0), ag(FRONT, 1)
    step(c0, c1)
    step(b0, b1)
    step(c0, c1)
    step(c0, c1)
    step(b0, b1)
    step(c0, c1)
    step(b0, b1)
    step(f0, f1)
    finish(b0, b1)
    step(f0, f1)
    step(c0, c1)
    step(f0, f1)
    step(f0, f1)
    step(c0, c1)
    step(f0, f1)
    step(c0, c1)
    finish(c0, c1)
    for copy in loads[:3]:
        copy.wait()
    r0, r1, q0, q1 = rs(0, 0), rs(0, 1), rs(1, 0), rs(1, 1)
    back_chunk(0)
    step(f0, f1)
    back_chunk(1)
    step(r0, r1, f0, f1)
    back_chunk(2)
    step(f0, f1)
    back_chunk(3)
    finish(f0, f1)
    step(r0, r1)
    for copy in pending[FRONT]:
        copy.wait_send()
    front_chunk(0)
    step(r0, r1)
    front_chunk(1)
    step(q0, q1, r0, r1)
    front_chunk(2)
    front_chunk(3)
    step(r0, r1)
    step(q0, q1)
    step(r0, r1)
    step(r0, r1)
    step(r0, r1)
    step(q0, q1)
    finish(r0, r1)
    for copy in loads[3:]:
        copy.wait()
    grad_tiles(0, 0, 4)
    step(q0, q1)
    grad_tiles(0, 4, 7)
    step(q0, q1)
    grad_tiles(1, 0, 4)
    step(q0, q1)
    grad_tiles(1, 4, 7)
    step(q0, q1)
    saves = [
        pltpu.make_async_copy(mg, o_gate, save_sem.at[0]),
        pltpu.make_async_copy(mu, o_up, save_sem.at[1]),
        pltpu.make_async_copy(md, o_down, save_sem.at[2]),
    ]
    for copy in saves:
        copy.start()

    values = saved[...].astype(F32)
    inverse = rinv_of(values)
    scaled = total_of(0) * gain[...].astype(F32)
    out_b[...] = (
        came_b[...].astype(F32)
        + inverse * scaled
        - inverse * inverse * inverse * values * jnp.mean(scaled * values, axis=-1, keepdims=True)
    ).astype(BF)
    finish(q0, q1)
    out_f[...] = (came_f[...].astype(F32) + total_of(1)).astype(BF)

    for copy in sec_copies:
        copy.wait_send()
    for copy in pending[ROWS_B] + pending[GRADS] + done:
        copy.wait_send()
    for copy in saves:
        copy.wait()


def body(*args):
    (fresh, sent_f, sent_b, turn, saved, gain, ids_f, aff_f, ids_b, aff_b,
     w_gate, w_up, w_down, m_gate, m_up, m_down) = args
    vmem = pl.BlockSpec(memory_space=pltpu.VMEM)
    hbm = pl.BlockSpec(memory_space=pl.ANY)
    sds = jax.ShapeDtypeStruct
    dma = pltpu.SemaphoreType.DMA
    outs = pl.pallas_call(
        kernel,
        out_shape=(
            sds((TOK, D), BF), sds((TOK, D), BF),
            sds((D, HID), BF), sds((D, HID), BF), sds((HID, D), BF),
        ),
        in_specs=[vmem] * 10 + [hbm] * 6,
        out_specs=(vmem, vmem, hbm, hbm, hbm),
        scratch_shapes=[
            pltpu.VMEM((3, 2, 4, 4, 2, TOK, W + 128), BF),
            pltpu.VMEM((3, 2, 4, 4, 2, TOK, W), BF),
            pltpu.VMEM((2, 2, 4, 4, 2, TOK, W), BF),
            pltpu.VMEM((4, 4, 4, 2, TOK, W), BF),
            pltpu.VMEM((4, 2, 3, 2, 2, TOK, W), BF),
            pltpu.VMEM((4, 2, 3, TOK, W), BF),
            pltpu.VMEM((4, TOK, W), BF),
            pltpu.VMEM((D, 2 * HID), BF),
            pltpu.VMEM((HID, D), BF),
            pltpu.VMEM((D, HID), BF),
            pltpu.VMEM((D, HID), BF),
            pltpu.VMEM((HID, D), BF),
            pltpu.VMEM((2 * HID, 1024), BF),
            pltpu.VMEM((HID, 1024), BF),
            pltpu.VMEM((TOK, D), BF),
            pltpu.VMEM((TOK, D), BF),
            dma((6 * N_AG,)), dma((6 * N_AG,)),
            dma((4 * N_RS,)), dma((4 * N_RS,)),
            dma((2,)), dma((2,)), dma((6,)), dma((3,)),
        ],
        compiler_params=pltpu.CompilerParams(
            collective_id=0, has_side_effects=True, vmem_limit_bytes=60 * 2**20
        ),
    )(
        fresh, sent_f[0], sent_b[0], turn, saved[0], gain, ids_f[0], aff_f[0], ids_b[0], aff_b[0],
        w_gate[0], w_up[0], w_down[0], m_gate[0], m_up[0], m_down[0],
    )
    return tuple(o[None] for o in outs)


def solution(mesh):
    rows = P("section", "ep", None)
    cols = P("section", None, "ep")
    return jax.shard_map(
        body,
        mesh=mesh,
        in_specs=(
            P("ep", None), rows, rows, P("ep", None), rows, P("section", None),
            rows, rows, rows, rows, cols, cols, rows, cols, cols, rows,
        ),
        out_specs=(rows, rows, cols, cols, rows),
        check_vma=False,
    )
```

```python
import functools
import jax
import jax.numpy as jnp
from jax import lax
from jax.experimental import pallas as pl
from jax.experimental.pallas import tpu as pltpu
from jax.sharding import PartitionSpec as P

BF = jnp.bfloat16
F32 = jnp.float32
MESH = pl.DeviceIdType.MESH
D = 3584
W = D // 2
TOK = 16
HID = 128
EXPERTS = 8
ROWS = 256
TILE = 256
CAP = 8
ROWS_B, GRADS, FRONT = 0, 1, 2
N_AG = 17
N_RS = 14


def kernel(
    fresh, sent_f, sent_b, turn, saved, gain, ids_f, aff_f, ids_b, aff_b,
    w_gate, w_up, w_down, m_gate, m_up, m_down,
    out_f, out_b, o_gate, o_up, o_down,
    tk, g0, g1, packed_y, packed_x, relay, part, core_in, slots_y, relay_back, slots_x,
    tokens, small_in, last_in, pick_y, pick_x, pick_y_t, pick_x_t,
    wgu, wd, mg, mu, md, dgu_t, hid_t, came_f, came_b,
    ag_send, ag_recv, rs_send, rs_recv, sec_send, sec_recv, load_sem, save_sem,
):
    sec = lax.axis_index("section")
    ep = lax.axis_index("ep")
    core = lax.rem(ep, 2)
    z = lax.rem(ep // 2, 2)
    x = lax.rem(ep // 4, 4)
    y = ep // 16
    expert = ep // 8
    pair = x // 2
    x_in = x + 1 - 2 * lax.rem(x, 2)

    def at(yy, xx, zz, cc):
        return (sec, ((yy * 4 + xx) * 2 + zz) * 2 + cc)

    def turn4(v, by):
        return lax.rem(v + by, 4)

    dev_z = at(y, x, 1 - z, core)
    dev_c = at(y, x, z, 1 - core)
    dev_y = (at(turn4(y, 1), x, z, core), at(turn4(y, 3), x, z, core))
    dev_x = (at(y, turn4(x, 1), z, core), at(y, turn4(x, 3), z, core))
    x_out = turn4(x, 3 + 2 * lax.rem(x, 2))
    x_far = turn4(x, 2)
    dev_in, dev_out = at(y, x_in, z, core), at(y, x_out, z, core)
    dev_s = ((turn4(sec, 1), ep), (turn4(sec, 3), ep))

    loads = [
        pltpu.make_async_copy(w_gate, wgu.at[:, pl.ds(0, HID)], load_sem.at[0]),
        pltpu.make_async_copy(w_up, wgu.at[:, pl.ds(HID, HID)], load_sem.at[1]),
        pltpu.make_async_copy(w_down, wd, load_sem.at[2]),
        pltpu.make_async_copy(m_gate, mg, load_sem.at[3]),
        pltpu.make_async_copy(m_up, mu, load_sem.at[4]),
        pltpu.make_async_copy(m_down, md, load_sem.at[5]),
    ]

    def remote(src, dst, send, recv, dev):
        return pltpu.make_async_remote_copy(
            src_ref=src, dst_ref=dst, send_sem=send, recv_sem=recv,
            device_id=dev, device_id_type=MESH,
        )

    every = slice(None)
    lane128 = lax.broadcasted_iota(jnp.int32, (128, 128), 1)
    row128 = lax.broadcasted_iota(jnp.int32, (128, 128), 0)
    route_of = (0, 0, 1)
    width_of = (W + 128, W, W + 128)

    def build_picks(u, s):
        route = route_of[u]
        aux = tk[s, u, :, :, :, pl.ds(W, 128)].reshape(128, 128)
        named = jnp.where((aux.astype(F32) > 0.0) & (lane128 < EXPERTS), 1.0, 0.0)
        before = jnp.where((row128 // TOK == lane128 // TOK) & (lane128 < row128), 1.0, 0.0)
        order = dot(before.astype(BF), named.astype(BF))
        block = lax.broadcasted_iota(jnp.int32, (128, 1), 0) // TOK

        def places(e):
            chosen = jnp.sum(jnp.where(lane128 == e, named, 0.0), axis=1, keepdims=True)
            slot = jnp.sum(jnp.where(lane128 == e, order, 0.0), axis=1, keepdims=True)
            return chosen, block * CAP + slot.astype(jnp.int32)

        if s == 0:
            wanted = [2 * turn4(y, r) + pair for r in range(4)]
        else:
            wanted = [2 * y + pair, 2 * y + 1 - pair]
        lane = lax.broadcasted_iota(jnp.int32, (128, 64 * len(wanted)), 1)
        pick = jnp.zeros((128, 64 * len(wanted)), F32)
        for r, e in enumerate(wanted):
            chosen, target = places(e)
            pick = pick + jnp.where(lane == target + 64 * r, chosen, 0.0)
        (pick_y, pick_x)[s][route] = pick.astype(BF)
        (pick_y_t, pick_x_t)[s][route] = pick.T.astype(BF)

    def pack(u, s):
        route = route_of[u]
        if u != GRADS:
            build_picks(u, s)

        def tile(lo, size):
            rows = tk[s, u, :, :, :, pl.ds(lo, size)].reshape(128, size)
            res = dot((pick_y_t, pick_x_t)[s][route], rows).astype(BF)
            if s == 0:
                g0[u, core, y, :, :, pl.ds(lo, size)] = res[:64].reshape(4, TOK, size)
                for r in range(3):
                    packed_y[u, r, :, :, pl.ds(lo, size)] = (
                        res[64 * (r + 1) : 64 * (r + 2)].reshape(4, TOK, size)
                    )
            else:
                g1[u, core, :, x, :, pl.ds(lo, size)] = res[:64].reshape(4, TOK, size)
                packed_x[u, :, :, pl.ds(lo, size)] = res[64:].reshape(4, TOK, size)

        @pl.loop(0, W // TILE)
        def _(n):
            tile(pl.multiple_of(n * TILE, TILE), TILE)

        if s == 0 and u != GRADS:
            tile(W, 128)

    pending = []

    def ag(u, s):
        base = (u * 2 + s) * N_AG

        def put(k, src, dst, dev):
            copy = remote(src, dst, ag_send.at[base + k], ag_recv.at[base + k], dev)
            copy.start()
            pending.append(copy)

        def got(k, ref):
            remote(ref, ref, ag_send.at[base + k], ag_recv.at[base + k], dev_c).wait_recv()

        me, dev = ((x, dev_x), (y, dev_y))[s]

        def blk(i, h):
            return tk.at[s, u, i, h, :, pl.ds(0, width_of[u])]

        def same(k, ref, to):
            put(k, ref, ref, to)

        same(0, blk(me, z), dev_z)
        yield
        got(0, blk(me, 1 - z))
        left, right, far = turn4(me, 3), turn4(me, 1), turn4(me, 2)
        same(1, blk(me, 0), dev[0])
        same(3, blk(me, 1), dev[1])
        same(2, blk(me, 1), dev[0])
        same(4, blk(me, 0), dev[1])
        yield
        got(1, blk(left, 0))
        same(5, blk(left, 0), dev[0])
        got(3, blk(right, 1))
        same(6, blk(right, 1), dev[1])
        yield
        got(2, blk(left, 1))
        got(4, blk(right, 0))
        yield
        got(5, blk(far, 0))
        got(6, blk(far, 1))
        pack(u, s)
        if s == 0:
            wide = pl.ds(0, width_of[u])

            def home(cc, yy, xx):
                return g0.at[u, cc, yy, xx, :, wide]

            low, high = pl.ds(0, 2), pl.ds(2, 2)
            up, down, over = turn4(y, 1), turn4(y, 3), turn4(y, 2)
            put(7, packed_y.at[u, 1, low, :, wide], relay.at[u, 0, :, :, wide], dev_y[0])
            put(8, packed_y.at[u, 1, high, :, wide], relay.at[u, 1, :, :, wide], dev_y[1])
            put(9, packed_y.at[u, 0, :, :, wide], home(core, y, every), dev_y[0])
            put(10, packed_y.at[u, 2, :, :, wide], home(core, y, every), dev_y[1])
            same(13, home(core, y, every), dev_c)
            yield
            got(7, relay.at[u, 0, :, :, wide])
            put(11, relay.at[u, 0, :, :, wide], home(core, down, low), dev_y[0])
            got(8, relay.at[u, 1, :, :, wide])
            put(12, relay.at[u, 1, :, :, wide], home(core, up, high), dev_y[1])
            yield
            got(9, home(core, down, every))
            same(14, home(core, down, every), dev_c)
            got(10, home(core, up, every))
            same(15, home(core, up, every), dev_c)
            yield
            got(11, home(core, over, low))
            got(12, home(core, over, high))
            same(16, home(core, over, every), dev_c)
            yield
            for k, i in ((13, y), (14, down), (15, up), (16, over)):
                got(k, home(1 - core, i, every))
        else:

            def home(cc, yy, xx):
                return g1.at[u, cc, yy, xx]

            low, high = pl.ds(0, 2), pl.ds(2, 2)
            put(7, packed_x.at[u, low], home(core, low, x), dev_out)
            same(9, home(core, every, x), dev_in)
            put(8, packed_x.at[u, high], home(core, high, x), dev_out)
            same(13, home(core, every, x), dev_c)
            yield
            got(7, home(core, low, x_out))
            same(10, home(core, low, x_out), dev_in)
            yield
            got(8, home(core, high, x_out))
            same(11, home(core, high, x_out), dev_in)
            same(14, home(core, every, x_out), dev_c)
            got(9, home(core, every, x_in))
            same(15, home(core, every, x_in), dev_c)
            yield
            got(10, home(core, low, x_far))
            got(11, home(core, high, x_far))
            same(16, home(core, every, x_far), dev_c)
            yield
            for k, i in ((13, x), (14, x_out), (15, x_in), (16, x_far)):
                got(k, home(1 - core, every, i))

    done = []

    def add_into(dst, *srcs):
        total = dst[...].astype(F32)
        for src in srcs:
            total = total + src[...].astype(F32)
        dst[...] = total.astype(BF)

    def rs(u, s):
        q = u * 2 + s
        base = q * N_RS

        def put(k, src, dst, dev):
            copy = remote(src, dst, rs_send.at[base + k], rs_recv.at[base + k], dev)
            copy.start()
            done.append(copy)

        def got(k, ref):
            remote(ref, ref, rs_send.at[base + k], rs_recv.at[base + k], dev_c).wait_recv()

        put(0, part.at[u, s, 1 - core], core_in.at[q], dev_c)
        yield
        got(0, core_in.at[q])

        @pl.loop(0, 4)
        def _(yy):
            for xx in range(4):
                add_into(part.at[u, s, core, yy, xx], core_in.at[q, yy, xx])

        if s == 0:
            low, high = pl.ds(0, 2), pl.ds(2, 2)
            up, down, over = turn4(y, 1), turn4(y, 3), turn4(y, 2)
            put(1, part.at[u, s, core, over, low], relay_back.at[u, 0], dev_y[0])
            put(2, part.at[u, s, core, over, high], relay_back.at[u, 1], dev_y[1])
            put(3, part.at[u, s, core, up], slots_y.at[u, 2], dev_y[0])
            put(4, part.at[u, s, core, down], slots_y.at[u, 0], dev_y[1])
            yield
            got(1, relay_back.at[u, 0])
            put(5, relay_back.at[u, 0], slots_y.at[u, 1, low], dev_y[0])
            got(2, relay_back.at[u, 1])
            put(6, relay_back.at[u, 1], slots_y.at[u, 1, high], dev_y[1])
            yield
            got(3, slots_y.at[u, 2])
            got(4, slots_y.at[u, 0])
            yield
            got(5, slots_y.at[u, 1, low])
            got(6, slots_y.at[u, 1, high])
        else:
            put(1, part.at[u, s, core, :, x_far], slots_x.at[u, 0], dev_in)
            put(2, part.at[u, s, core, :, x_in], slots_x.at[u, 1], dev_in)
            yield
            got(1, slots_x.at[u, 0])
            add_each(part.at[u, s, core, :, x_out], slots_x.at[u, 0])
            put(3, part.at[u, s, core, :, x_out], slots_x.at[u, 2], dev_out)
            yield
            got(2, slots_x.at[u, 1])
            add_each(part.at[u, s, core, :, x], slots_x.at[u, 1])
            yield
            got(3, slots_x.at[u, 2])

        @pl.loop(0, W // TILE)
        def _(n):
            here = pl.ds(pl.multiple_of(n * TILE, TILE), TILE)
            if s == 0:
                pick = pick_y[u]
                rows = [part[u, s, core, y, :, :, here].reshape(64, TILE)] + [
                    slots_y[u, r, :, :, here].reshape(64, TILE) for r in range(3)
                ]
            else:
                pick = pick_x[u]
                rows = [
                    part[u, s, core, :, x, :, here].reshape(64, TILE),
                    slots_x[u, 2, :, :, here].reshape(64, TILE),
                ]
            res = dot(pick, jnp.concatenate(rows, axis=0)).astype(BF)
            tokens[q, :, :, :, here] = res.reshape(4, 2, TOK, TILE)

        me, dev = ((x, dev_x), (y, dev_y))[s]
        left, right, far = turn4(me, 3), turn4(me, 1), turn4(me, 2)

        def blk(i, h):
            return tokens.at[q, i, h]

        def buf(d, j):
            return small_in.at[q, d, j]

        put(7, blk(far, 0), buf(0, 0), dev[0])
        put(8, blk(far, 1), buf(1, 0), dev[1])
        put(9, blk(right, 1), buf(0, 2), dev[0])
        put(10, blk(left, 0), buf(1, 1), dev[1])
        yield
        got(7, buf(0, 0))
        add_into(blk(right, 0), buf(0, 0))
        put(11, blk(right, 0), buf(0, 1), dev[0])
        got(8, buf(1, 0))
        add_into(blk(left, 1), buf(1, 0))
        put(12, blk(left, 1), buf(1, 2), dev[1])
        yield
        got(9, buf(0, 2))
        got(10, buf(1, 1))
        yield
        got(11, buf(0, 1))
        got(12, buf(1, 2))
        add_into(blk(me, 0), buf(0, 1), buf(1, 1))
        add_into(blk(me, 1), buf(0, 2), buf(1, 2))
        put(13, blk(me, 1 - z), last_in.at[q], dev_z)
        yield
        got(13, last_in.at[q])

    def add_each(dst, src):
        for i in range(4):
            add_into(dst.at[i], src.at[i])

    def total_of(u):
        halves = [
            tokens[u * 2 + s, (x, y)[s], z].astype(F32) + last_in[u * 2 + s].astype(F32)
            for s in range(2)
        ]
        return jnp.concatenate(halves, axis=1)

    def rinv_of(v):
        return lax.rsqrt(jnp.mean(v * v, axis=-1, keepdims=True) + 1e-6)

    def place(u, value, weights=None):
        tk[0, u, x, z, :, pl.ds(0, W)] = value[:, :W]
        tk[1, u, y, z, :, pl.ds(0, W)] = value[:, W:]
        if weights is not None:
            tk[0, u, x, z, :, pl.ds(W, 128)] = weights
            tk[1, u, y, z, :, pl.ds(W, 128)] = weights

    def norm(ref):
        v = ref.astype(F32)
        return (v * rinv_of(v) * gain[...].astype(F32)).astype(BF)

    def weights_of(ids, aff):
        lane = lax.broadcasted_iota(jnp.int32, (TOK, 128), 1)
        eye = lax.broadcasted_iota(jnp.int32, (TOK, TOK), 0) == lax.broadcasted_iota(
            jnp.int32, (TOK, TOK), 1
        )

        def column(row):
            wide = jnp.broadcast_to(row.astype(F32), (TOK, TOK))
            return jnp.sum(jnp.where(eye, wide, 0.0), axis=1, keepdims=True)

        named = [column(ids[k : k + 1, :]).astype(jnp.int32) for k in range(2)]
        both = [column(aff[k : k + 1, :]) for k in range(2)]
        out = jnp.zeros((TOK, 128), F32)
        for k in range(2):
            one = both[k] / (both[0] + both[1])
            high = one.astype(BF).astype(F32)
            out = out + jnp.where(lane == named[k], high, 0.0)
            out = out + jnp.where(lane == named[k] + EXPERTS, one - high, 0.0)
        return out.astype(BF)

    def rows_of(u, cc):
        a = g0[u, cc, :, :, :, pl.ds(0, W)].reshape(ROWS, W)
        b = g1[u, cc].reshape(ROWS, W)
        return a, b

    def share_of(u, cc):
        aux = g0[u, cc, :, :, :, pl.ds(W, 128)].reshape(ROWS, 128).astype(F32)
        lane = lax.broadcasted_iota(jnp.int32, (ROWS, 128), 1)
        mine = (lane == expert) | (lane == expert + EXPERTS)
        return jnp.sum(jnp.where(mine, aux, 0.0), axis=1, keepdims=True)

    def dot(a, b):
        return jnp.dot(a, b, preferred_element_type=F32)

    def dot_t(a, b):
        return lax.dot_general(a, b, (((1,), (1,)), ((), ())), preferred_element_type=F32)

    def pre_acts(u, i):
        a, b = rows_of(u, i)
        gu = dot(a, wgu[pl.ds(0, W)]) + dot(b, wgu[pl.ds(W, W)])
        return gu[:, :HID], gu[:, HID:]

    def front_chunk(i):
        cc = (1 - core, core)[i]
        gate, up = pre_acts(FRONT, cc)
        hidden = (gate * jax.nn.sigmoid(gate) * up * share_of(FRONT, cc)).astype(BF)
        for s in range(2):
            @pl.loop(0, W // TILE)
            def _(n):
                lo = pl.multiple_of(n * TILE, TILE)
                res = dot(hidden, wd[:, pl.ds(s * W + lo, TILE)])
                part[1, s, cc, :, :, :, pl.ds(lo, TILE)] = res.astype(BF).reshape(4, 4, TOK, TILE)

    def back_chunk(i):
        cc = (1 - core, core)[i]
        gate, up = pre_acts(ROWS_B, cc)
        a, b = rows_of(GRADS, cc)
        share = share_of(ROWS_B, cc)
        sig = jax.nn.sigmoid(gate)
        active = gate * sig
        grad_hidden = (dot_t(a, wd[:, pl.ds(0, W)]) + dot_t(b, wd[:, pl.ds(W, W)])) * share
        dgate = grad_hidden * up * sig * (1.0 + gate * (1.0 - sig))
        dup = grad_hidden * active
        scaled = active * up * share
        lo = pl.multiple_of(cc * ROWS, ROWS)
        dgu_t[pl.ds(0, HID), pl.ds(lo, ROWS)] = dgate.T.astype(BF)
        dgu_t[pl.ds(HID, HID), pl.ds(lo, ROWS)] = dup.T.astype(BF)
        hid_t[:, pl.ds(lo, ROWS)] = scaled.T.astype(BF)
        both = jnp.concatenate([dgate, dup], axis=1).astype(BF)
        for s in range(2):
            @pl.loop(0, W // TILE)
            def _(n):
                lo = pl.multiple_of(n * TILE, TILE)
                res = dot_t(both, wgu[pl.ds(s * W + lo, TILE)])
                part[0, s, cc, :, :, :, pl.ds(lo, TILE)] = res.astype(BF).reshape(4, 4, TOK, TILE)

    def grad_tiles(s, first, last):
        @pl.loop(first, last)
        def _(n):
            lo = pl.multiple_of(n * TILE, TILE)
            g = (g0, g1)[s]
            rows = g[ROWS_B, :, :, :, :, pl.ds(lo, TILE)].reshape(2 * ROWS, TILE)
            here = pl.ds(s * W + lo, TILE)
            res = dot(dgu_t[...], rows)
            mg[here] = (mg[here].astype(F32) + res[:HID].T).astype(BF)
            mu[here] = (mu[here].astype(F32) + res[HID:].T).astype(BF)
            cot = g[GRADS, :, :, :, :, pl.ds(lo, TILE)].reshape(2 * ROWS, TILE)
            md[:, here] = (md[:, here].astype(F32) + dot(hid_t[...], cot)).astype(BF)

    def step(*gens):
        for g in gens:
            next(g, None)

    def finish(*gens):
        for g in gens:
            for _ in g:
                pass

    barrier = pltpu.get_barrier_semaphore()
    for dev in (dev_z, dev_c, *dev_y, *dev_x, *dev_s):
        pl.semaphore_signal(barrier, inc=1, device_id=dev, device_id_type=MESH)
    pl.semaphore_wait(barrier, 8)

    sec_copies = [
        remote(sent_b, came_b, sec_send.at[0], sec_recv.at[0], dev_s[1]),
        remote(sent_f, came_f, sec_send.at[1], sec_recv.at[1], dev_s[0]),
    ]
    for copy in sec_copies:
        copy.start()
    weights_b = weights_of(ids_b, aff_b)
    place(ROWS_B, norm(saved[...]), weights_b)
    b = ag(ROWS_B, 0), ag(ROWS_B, 1)
    c = ag(GRADS, 0), ag(GRADS, 1)
    f = ag(FRONT, 0), ag(FRONT, 1)
    r = rs(0, 0), rs(0, 1)
    q = rs(1, 0), rs(1, 1)
    step(*b)
    for copy in loads:
        copy.start()
    step(*b)
    weights_f = weights_of(ids_f, aff_f)
    step(*b)
    step(*b)
    step(*b)
    sec_copies[0].wait_recv()
    upstream = jnp.where(sec == 3, turn[...], came_b[...])
    came_b[...] = upstream
    place(GRADS, upstream)
    step(*c)
    sec_copies[1].wait_recv()
    front = jnp.where(sec == 0, fresh[...], came_f[...])
    came_f[...] = front
    place(FRONT, norm(front), weights_f)
    step(*b)
    step(*c)
    step(*c)
    step(*b)
    step(*c)
    step(*c)
    step(*f)
    step(*b)
    step(*f)
    step(*c)
    step(*f)
    step(*c)
    step(*f)
    step(*f)
    step(*c)
    finish(*b)
    finish(*c)
    for copy in loads[:3]:
        copy.wait()
    step(*f)
    back_chunk(0)
    step(*f, *r)
    back_chunk(1)
    finish(*f)
    step(*r)
    front_chunk(0)
    step(*q, *r)
    front_chunk(1)
    step(*r)
    step(*q)
    step(*r)
    step(*r)
    step(*r)
    step(*q)
    finish(*r)
    for copy in loads[3:]:
        copy.wait()
    grad_tiles(0, 0, 7)
    step(*q)
    grad_tiles(1, 0, 7)
    step(*q)
    step(*q)
    step(*q)
    step(*q)
    saves = [
        pltpu.make_async_copy(mg, o_gate, save_sem.at[0]),
        pltpu.make_async_copy(mu, o_up, save_sem.at[1]),
        pltpu.make_async_copy(md, o_down, save_sem.at[2]),
    ]
    for copy in saves:
        copy.start()

    values = saved[...].astype(F32)
    inverse = rinv_of(values)
    scaled = total_of(0) * gain[...].astype(F32)
    out_b[...] = (
        came_b[...].astype(F32)
        + inverse * scaled
        - inverse * inverse * inverse * values * jnp.mean(scaled * values, axis=-1, keepdims=True)
    ).astype(BF)
    finish(*q)
    out_f[...] = (came_f[...].astype(F32) + total_of(1)).astype(BF)

    for copy in sec_copies:
        copy.wait_send()
    for copy in pending + done:
        copy.wait_send()
    for copy in saves:
        copy.wait()


def hand_over(*refs):
    held, came, went = refs[10:15], refs[15], refs[16]
    order = (2, 3, 4, 0, 1)
    ins = {i: pltpu.make_async_copy(refs[i], held[i], came.at[i]) for i in order}
    outs = {i: pltpu.make_async_copy(held[i], refs[5 + i].at[0], went.at[i]) for i in order}
    for i in order:
        ins[i].start()
    for i in order:
        ins[i].wait()
        outs[i].start()
    for i in order:
        outs[i].wait()


def body(*args):
    (fresh, sent_f, sent_b, turn, saved, gain, ids_f, aff_f, ids_b, aff_b,
     w_gate, w_up, w_down, m_gate, m_up, m_down) = args
    vmem = pl.BlockSpec(memory_space=pltpu.VMEM)
    hbm = pl.BlockSpec(memory_space=pl.ANY)
    sds = jax.ShapeDtypeStruct
    dma = pltpu.SemaphoreType.DMA
    outs = pl.pallas_call(
        kernel,
        out_shape=(
            sds((TOK, D), BF), sds((TOK, D), BF),
            sds((D, HID), BF), sds((D, HID), BF), sds((HID, D), BF),
        ),
        in_specs=[vmem] * 10 + [hbm] * 6,
        out_specs=(vmem, vmem, hbm, hbm, hbm),
        scratch_shapes=[
            pltpu.VMEM((2, 3, 4, 2, TOK, W + 128), BF),
            pltpu.VMEM((3, 2, 4, 4, TOK, W + 128), BF),
            pltpu.VMEM((3, 2, 4, 4, TOK, W), BF),
            pltpu.VMEM((3, 3, 4, TOK, W + 128), BF),
            pltpu.VMEM((3, 4, TOK, W), BF),
            pltpu.VMEM((3, 2, 2, TOK, W + 128), BF),
            pltpu.VMEM((2, 2, 2, 4, 4, TOK, W), BF),
            pltpu.VMEM((4, 4, 4, TOK, W), BF),
            pltpu.VMEM((2, 3, 4, TOK, W), BF),
            pltpu.VMEM((2, 2, 2, TOK, W), BF),
            pltpu.VMEM((2, 3, 4, TOK, W), BF),
            pltpu.VMEM((4, 4, 2, TOK, W), BF),
            pltpu.VMEM((4, 2, 3, TOK, W), BF),
            pltpu.VMEM((4, TOK, W), BF),
            pltpu.VMEM((2, 128, 256), BF),
            pltpu.VMEM((2, 128, 128), BF),
            pltpu.VMEM((2, 256, 128), BF),
            pltpu.VMEM((2, 128, 128), BF),
            pltpu.VMEM((D, 2 * HID), BF),
            pltpu.VMEM((HID, D), BF),
            pltpu.VMEM((D, HID), BF),
            pltpu.VMEM((D, HID), BF),
            pltpu.VMEM((HID, D), BF),
            pltpu.VMEM((2 * HID, 2 * ROWS), BF),
            pltpu.VMEM((HID, 2 * ROWS), BF),
            pltpu.VMEM((TOK, D), BF),
            pltpu.VMEM((TOK, D), BF),
            dma((6 * N_AG,)), dma((6 * N_AG,)),
            dma((4 * N_RS,)), dma((4 * N_RS,)),
            dma((2,)), dma((2,)), dma((6,)), dma((3,)),
        ],
        compiler_params=pltpu.CompilerParams(
            collective_id=0, has_side_effects=True, vmem_limit_bytes=60 * 2**20
        ),
    )(
        fresh, sent_f[0], sent_b[0], turn, saved[0], gain, ids_f[0].T, aff_f[0].T, ids_b[0].T, aff_b[0].T,
        w_gate[0], w_up[0], w_down[0], m_gate[0], m_up[0], m_down[0],
    )
    return pl.pallas_call(
        hand_over,
        out_shape=tuple(sds((1, *o.shape), BF) for o in outs),
        in_specs=[hbm] * 5,
        out_specs=(hbm,) * 5,
        scratch_shapes=[*(pltpu.VMEM(o.shape, BF) for o in outs), dma((5,)), dma((5,))],
    )(*outs)


def solution(mesh):
    rows = P("section", "ep", None)
    cols = P("section", None, "ep")
    return jax.shard_map(
        body,
        mesh=mesh,
        in_specs=(
            P("ep", None), rows, rows, P("ep", None), rows, P("section", None),
            rows, rows, rows, rows, cols, cols, rows, cols, cols, rows,
        ),
        out_specs=(rows, rows, cols, cols, rows),
        check_vma=False,
    )
```

```python
import functools
import jax
import jax.numpy as jnp
from jax import lax
from jax.experimental import pallas as pl
from jax.experimental.pallas import tpu as pltpu
from jax.sharding import PartitionSpec as P

BF = jnp.bfloat16
F32 = jnp.float32
MESH = pl.DeviceIdType.MESH
D = 3584
W = D // 2
TOK = 16
HID = 128
EXPERTS = 8
ROWS = 256
TILE = 256
CAP = 8
ROWS_B, GRADS, FRONT = 0, 1, 2
N_AG = 17
ORDER = (
    "enter", "b", "sec", "load", "b", "b", "C", "c", "F", "f", "b", "b", "c", "f", "c", "f",
    "b", "c", "f", "c", "b", "f", "b", "c", "W", "b", "P0", "c", "P1", "c", "c", "f",
    "K0", "f", "r", "K1", "r", "f", "f", "H0", "q", "r", "H1", "q", "r", "r", "q", "r",
    "q", "M", "G0", "r", "q", "r", "q", "G1", "r", "eb", "G2", "q", "G3", "G4", "q", "G5",
    "save", "ws", "wr", "q", "ef",
)
N_RS = 14


def kernel(
    fresh_in, sent_f, sent_b, turn_in, saved_in, gain_in, ids_f_in, aff_f_in, ids_b_in, aff_b_in,
    w_gate, w_up, w_down, m_gate, m_up, m_down,
    out_f, out_b, o_gate, o_up, o_down,
    tk, g0, g1, packed_y, packed_x, relay, part, core_in, slots_y, relay_back, slots_x,
    tokens, small_in, last_in, pick_y, pick_x, pick_y_t, pick_x_t,
    wgu, wd, mg, mu, md, dgu_t, hid_t, acts, came_f, came_b,
    fresh, turn, saved, gain, ids_f, aff_f, ids_b, aff_b,
    ag_send, ag_recv, rs_send, rs_recv, sec_send, sec_recv, load_sem, save_sem, in_sem,
):
    sec = lax.axis_index("section")
    ep = lax.axis_index("ep")
    core = lax.rem(ep, 2)
    z = lax.rem(ep // 2, 2)
    x = lax.rem(ep // 4, 4)
    y = ep // 16
    expert = ep // 8
    pair = x // 2
    x_in = x + 1 - 2 * lax.rem(x, 2)

    def at(yy, xx, zz, cc):
        return (sec, ((yy * 4 + xx) * 2 + zz) * 2 + cc)

    def turn4(v, by):
        return lax.rem(v + by, 4)

    dev_z = at(y, x, 1 - z, core)
    dev_c = at(y, x, z, 1 - core)
    dev_y = (at(turn4(y, 1), x, z, core), at(turn4(y, 3), x, z, core))
    dev_x = (at(y, turn4(x, 1), z, core), at(y, turn4(x, 3), z, core))
    x_out = turn4(x, 3 + 2 * lax.rem(x, 2))
    x_far = turn4(x, 2)
    dev_in, dev_out = at(y, x_in, z, core), at(y, x_out, z, core)
    dev_s = ((turn4(sec, 1), ep), (turn4(sec, 3), ep))

    loads = [
        pltpu.make_async_copy(w_gate, wgu.at[:, pl.ds(0, HID)], load_sem.at[0]),
        pltpu.make_async_copy(w_up, wgu.at[:, pl.ds(HID, HID)], load_sem.at[1]),
        pltpu.make_async_copy(w_down, wd, load_sem.at[2]),
        pltpu.make_async_copy(m_gate, mg, load_sem.at[3]),
        pltpu.make_async_copy(m_up, mu, load_sem.at[4]),
        pltpu.make_async_copy(m_down, md, load_sem.at[5]),
    ]

    def remote(src, dst, send, recv, dev):
        return pltpu.make_async_remote_copy(
            src_ref=src, dst_ref=dst, send_sem=send, recv_sem=recv,
            device_id=dev, device_id_type=MESH,
        )

    every = slice(None)
    lane128 = lax.broadcasted_iota(jnp.int32, (128, 128), 1)
    row128 = lax.broadcasted_iota(jnp.int32, (128, 128), 0)
    route_of = (0, 0, 1)
    width_of = (W + 128, W, W + 128)

    def build_picks(u, s):
        route = route_of[u]
        aux = tk[s, u, :, :, :, pl.ds(W, 128)].reshape(128, 128)
        named = jnp.where((aux.astype(F32) > 0.0) & (lane128 < EXPERTS), 1.0, 0.0)
        before = jnp.where((row128 // TOK == lane128 // TOK) & (lane128 < row128), 1.0, 0.0)
        order = dot(before.astype(BF), named.astype(BF))
        block = lax.broadcasted_iota(jnp.int32, (128, 1), 0) // TOK

        def places(e):
            chosen = jnp.sum(jnp.where(lane128 == e, named, 0.0), axis=1, keepdims=True)
            slot = jnp.sum(jnp.where(lane128 == e, order, 0.0), axis=1, keepdims=True)
            return chosen, block * CAP + slot.astype(jnp.int32)

        if s == 0:
            wanted = [2 * turn4(y, r) + pair for r in range(4)]
        else:
            wanted = [2 * y + pair, 2 * y + 1 - pair]
        lane = lax.broadcasted_iota(jnp.int32, (128, 64 * len(wanted)), 1)
        pick = jnp.zeros((128, 64 * len(wanted)), F32)
        for r, e in enumerate(wanted):
            chosen, target = places(e)
            pick = pick + jnp.where(lane == target + 64 * r, chosen, 0.0)
        (pick_y, pick_x)[s][route] = pick.astype(BF)
        (pick_y_t, pick_x_t)[s][route] = pick.T.astype(BF)

    def pack(u, s):
        route = route_of[u]
        if u != GRADS:
            build_picks(u, s)

        def tile(lo, size):
            rows = tk[s, u, :, :, :, pl.ds(lo, size)].reshape(128, size)
            res = dot((pick_y_t, pick_x_t)[s][route], rows).astype(BF)
            if s == 0:
                g0[u, core, y, :, :, pl.ds(lo, size)] = res[:64].reshape(4, TOK, size)
                for r in range(3):
                    packed_y[u, r, :, :, pl.ds(lo, size)] = (
                        res[64 * (r + 1) : 64 * (r + 2)].reshape(4, TOK, size)
                    )
            else:
                g1[u, core, :, x, :, pl.ds(lo, size)] = res[:64].reshape(4, TOK, size)
                packed_x[u, :, :, pl.ds(lo, size)] = res[64:].reshape(4, TOK, size)

        @pl.loop(0, W // TILE)
        def _(n):
            tile(pl.multiple_of(n * TILE, TILE), TILE)

        if s == 0 and u != GRADS:
            tile(W, 128)

    pending = []

    def ag(u, s):
        base = (u * 2 + s) * N_AG

        def put(k, src, dst, dev):
            copy = remote(src, dst, ag_send.at[base + k], ag_recv.at[base + k], dev)
            copy.start()
            pending.append(copy)

        def got(k, ref):
            remote(ref, ref, ag_send.at[base + k], ag_recv.at[base + k], dev_c).wait_recv()

        me, dev = ((x, dev_x), (y, dev_y))[s]

        def blk(i, h):
            return tk.at[s, u, i, h, :, pl.ds(0, width_of[u])]

        def same(k, ref, to):
            put(k, ref, ref, to)

        left, right, far = turn4(me, 3), turn4(me, 1), turn4(me, 2)
        same(0, blk(me, z), dev_z)
        same(1, blk(me, z), dev[0])
        same(3, blk(me, z), dev[1])
        yield
        got(0, blk(me, 1 - z))
        same(2, blk(me, 1 - z), dev[0])
        same(4, blk(me, 1 - z), dev[1])
        yield
        got(1, blk(left, z))
        same(5, blk(left, z), dev[0])
        got(4, blk(right, 1 - z))
        same(6, blk(right, 1 - z), dev[1])
        yield
        got(2, blk(left, 1 - z))
        got(3, blk(right, z))
        yield
        got(5, blk(far, z))
        got(6, blk(far, 1 - z))
        pack(u, s)
        if s == 0:
            wide = pl.ds(0, width_of[u])

            def home(cc, yy, xx):
                return g0.at[u, cc, yy, xx, :, wide]

            low, high = pl.ds(0, 2), pl.ds(2, 2)
            up, down, over = turn4(y, 1), turn4(y, 3), turn4(y, 2)
            put(7, packed_y.at[u, 1, low, :, wide], relay.at[u, 0, :, :, wide], dev_y[0])
            put(8, packed_y.at[u, 1, high, :, wide], relay.at[u, 1, :, :, wide], dev_y[1])
            put(9, packed_y.at[u, 0, :, :, wide], home(core, y, every), dev_y[0])
            put(10, packed_y.at[u, 2, :, :, wide], home(core, y, every), dev_y[1])
            same(13, home(core, y, every), dev_c)
            yield
            got(7, relay.at[u, 0, :, :, wide])
            put(11, relay.at[u, 0, :, :, wide], home(core, down, low), dev_y[0])
            got(8, relay.at[u, 1, :, :, wide])
            put(12, relay.at[u, 1, :, :, wide], home(core, up, high), dev_y[1])
            yield
            got(9, home(core, down, every))
            same(14, home(core, down, every), dev_c)
            got(10, home(core, up, every))
            same(15, home(core, up, every), dev_c)
            yield
            got(11, home(core, over, low))
            got(12, home(core, over, high))
            same(16, home(core, over, every), dev_c)
            yield
            for k, i in ((13, y), (14, down), (15, up), (16, over)):
                got(k, home(1 - core, i, every))
        else:

            def home(cc, yy, xx):
                return g1.at[u, cc, yy, xx]

            low, high = pl.ds(0, 2), pl.ds(2, 2)
            put(7, packed_x.at[u, low], home(core, low, x), dev_out)
            same(9, home(core, every, x), dev_in)
            put(8, packed_x.at[u, high], home(core, high, x), dev_out)
            same(13, home(core, every, x), dev_c)
            yield
            got(7, home(core, low, x_out))
            same(10, home(core, low, x_out), dev_in)
            yield
            got(8, home(core, high, x_out))
            same(11, home(core, high, x_out), dev_in)
            same(14, home(core, every, x_out), dev_c)
            got(9, home(core, every, x_in))
            same(15, home(core, every, x_in), dev_c)
            yield
            got(10, home(core, low, x_far))
            got(11, home(core, high, x_far))
            same(16, home(core, every, x_far), dev_c)
            yield
            for k, i in ((13, x), (14, x_out), (15, x_in), (16, x_far)):
                got(k, home(1 - core, every, i))

    done = []

    def add_into(dst, *srcs):
        total = dst[...].astype(F32)
        for src in srcs:
            total = total + src[...].astype(F32)
        dst[...] = total.astype(BF)

    def rs(u, s):
        q = u * 2 + s
        base = q * N_RS

        def put(k, src, dst, dev):
            copy = remote(src, dst, rs_send.at[base + k], rs_recv.at[base + k], dev)
            copy.start()
            done.append(copy)

        def got(k, ref):
            remote(ref, ref, rs_send.at[base + k], rs_recv.at[base + k], dev_c).wait_recv()

        put(0, part.at[u, s, 1 - core], core_in.at[q], dev_c)
        yield
        got(0, core_in.at[q])

        @pl.loop(0, 4)
        def _(yy):
            for xx in range(4):
                add_into(part.at[u, s, core, yy, xx], core_in.at[q, yy, xx])

        if s == 0:
            low, high = pl.ds(0, 2), pl.ds(2, 2)
            up, down, over = turn4(y, 1), turn4(y, 3), turn4(y, 2)
            put(1, part.at[u, s, core, over, low], relay_back.at[u, 0], dev_y[0])
            put(2, part.at[u, s, core, over, high], relay_back.at[u, 1], dev_y[1])
            put(3, part.at[u, s, core, up], slots_y.at[u, 2], dev_y[0])
            put(4, part.at[u, s, core, down], slots_y.at[u, 0], dev_y[1])
            yield
            got(1, relay_back.at[u, 0])
            put(5, relay_back.at[u, 0], slots_y.at[u, 1, low], dev_y[0])
            got(2, relay_back.at[u, 1])
            put(6, relay_back.at[u, 1], slots_y.at[u, 1, high], dev_y[1])
            yield
            got(3, slots_y.at[u, 2])
            got(4, slots_y.at[u, 0])
            yield
            got(5, slots_y.at[u, 1, low])
            got(6, slots_y.at[u, 1, high])
        else:
            put(1, part.at[u, s, core, :, x_far], slots_x.at[u, 0], dev_in)
            put(2, part.at[u, s, core, :, x_in], slots_x.at[u, 1], dev_in)
            yield
            got(1, slots_x.at[u, 0])
            add_each(part.at[u, s, core, :, x_out], slots_x.at[u, 0])
            put(3, part.at[u, s, core, :, x_out], slots_x.at[u, 2], dev_out)
            yield
            got(2, slots_x.at[u, 1])
            add_each(part.at[u, s, core, :, x], slots_x.at[u, 1])
            yield
            got(3, slots_x.at[u, 2])

        @pl.loop(0, W // TILE)
        def _(n):
            here = pl.ds(pl.multiple_of(n * TILE, TILE), TILE)
            if s == 0:
                pick = pick_y[u]
                rows = [part[u, s, core, y, :, :, here].reshape(64, TILE)] + [
                    slots_y[u, r, :, :, here].reshape(64, TILE) for r in range(3)
                ]
            else:
                pick = pick_x[u]
                rows = [
                    part[u, s, core, :, x, :, here].reshape(64, TILE),
                    slots_x[u, 2, :, :, here].reshape(64, TILE),
                ]
            res = dot(pick, jnp.concatenate(rows, axis=0)).astype(BF)
            tokens[q, :, :, :, here] = res.reshape(4, 2, TOK, TILE)

        me, dev = ((x, dev_x), (y, dev_y))[s]
        left, right, far = turn4(me, 3), turn4(me, 1), turn4(me, 2)

        def blk(i, h):
            return tokens.at[q, i, h]

        def buf(d, j):
            return small_in.at[q, d, j]

        put(7, blk(far, 0), buf(0, 0), dev[0])
        put(8, blk(far, 1), buf(1, 0), dev[1])
        put(9, blk(right, 1), buf(0, 2), dev[0])
        put(10, blk(left, 0), buf(1, 1), dev[1])
        yield
        got(7, buf(0, 0))
        add_into(blk(right, 0), buf(0, 0))
        put(11, blk(right, 0), buf(0, 1), dev[0])
        got(8, buf(1, 0))
        add_into(blk(left, 1), buf(1, 0))
        put(12, blk(left, 1), buf(1, 2), dev[1])
        yield
        got(9, buf(0, 2))
        got(10, buf(1, 1))
        yield
        got(11, buf(0, 1))
        got(12, buf(1, 2))
        add_into(blk(me, 0), buf(0, 1), buf(1, 1))
        add_into(blk(me, 1), buf(0, 2), buf(1, 2))
        put(13, blk(me, 1 - z), last_in.at[q], dev_z)
        yield
        got(13, last_in.at[q])

    def add_each(dst, src):
        for i in range(4):
            add_into(dst.at[i], src.at[i])

    def total_of(u):
        halves = [
            tokens[u * 2 + s, (x, y)[s], z].astype(F32) + last_in[u * 2 + s].astype(F32)
            for s in range(2)
        ]
        return jnp.concatenate(halves, axis=1)

    def rinv_of(v):
        return lax.rsqrt(jnp.mean(v * v, axis=-1, keepdims=True) + 1e-6)

    def place(u, value, weights=None):
        tk[0, u, x, z, :, pl.ds(0, W)] = value[:, :W]
        tk[1, u, y, z, :, pl.ds(0, W)] = value[:, W:]
        if weights is not None:
            tk[0, u, x, z, :, pl.ds(W, 128)] = weights
            tk[1, u, y, z, :, pl.ds(W, 128)] = weights

    def norm(ref):
        v = ref.astype(F32)
        return (v * rinv_of(v) * gain[...].astype(F32)).astype(BF)

    def weights_of(ids, aff):
        lane = lax.broadcasted_iota(jnp.int32, (TOK, 128), 1)
        eye = lax.broadcasted_iota(jnp.int32, (TOK, TOK), 0) == lax.broadcasted_iota(
            jnp.int32, (TOK, TOK), 1
        )

        def column(row):
            wide = jnp.broadcast_to(row.astype(F32), (TOK, TOK))
            return jnp.sum(jnp.where(eye, wide, 0.0), axis=1, keepdims=True)

        named = [column(ids[k : k + 1, :]).astype(jnp.int32) for k in range(2)]
        both = [column(aff[k : k + 1, :]) for k in range(2)]
        out = jnp.zeros((TOK, 128), F32)
        for k in range(2):
            one = both[k] / (both[0] + both[1])
            high = one.astype(BF).astype(F32)
            out = out + jnp.where(lane == named[k], high, 0.0)
            out = out + jnp.where(lane == named[k] + EXPERTS, one - high, 0.0)
        return out.astype(BF)

    def rows_of(u, cc):
        a = g0[u, cc, :, :, :, pl.ds(0, W)].reshape(ROWS, W)
        b = g1[u, cc].reshape(ROWS, W)
        return a, b

    def share_of(u, cc):
        aux = g0[u, cc, :, :, :, pl.ds(W, 128)].reshape(ROWS, 128).astype(F32)
        lane = lax.broadcasted_iota(jnp.int32, (ROWS, 128), 1)
        mine = (lane == expert) | (lane == expert + EXPERTS)
        return jnp.sum(jnp.where(mine, aux, 0.0), axis=1, keepdims=True)

    def dot(a, b):
        return jnp.dot(a, b, preferred_element_type=F32)

    def dot_t(a, b):
        return lax.dot_general(a, b, (((1,), (1,)), ((), ())), preferred_element_type=F32)

    def pre_acts(u, cc):
        a, b = rows_of(u, cc)
        return dot(a, wgu[pl.ds(0, W)]) + dot(b, wgu[pl.ds(W, W)])

    def back_acts(i):
        acts[i] = pre_acts(ROWS_B, (1 - core, core)[i])

    def front_chunk(i):
        cc = (1 - core, core)[i]
        both = pre_acts(FRONT, cc)
        gate, up = both[:, :HID], both[:, HID:]
        hidden = (gate * jax.nn.sigmoid(gate) * up * share_of(FRONT, cc)).astype(BF)
        for s in range(2):
            @pl.loop(0, W // TILE)
            def _(n):
                lo = pl.multiple_of(n * TILE, TILE)
                res = dot(hidden, wd[:, pl.ds(s * W + lo, TILE)])
                part[1, s, cc, :, :, :, pl.ds(lo, TILE)] = res.astype(BF).reshape(4, 4, TOK, TILE)

    def back_chunk(i):
        cc = (1 - core, core)[i]
        gate, up = acts[i, :, :HID], acts[i, :, HID:]
        a, b = rows_of(GRADS, cc)
        share = share_of(ROWS_B, cc)
        sig = jax.nn.sigmoid(gate)
        active = gate * sig
        grad_hidden = (dot_t(a, wd[:, pl.ds(0, W)]) + dot_t(b, wd[:, pl.ds(W, W)])) * share
        dgate = grad_hidden * up * sig * (1.0 + gate * (1.0 - sig))
        dup = grad_hidden * active
        scaled = active * up * share
        lo = pl.multiple_of(cc * ROWS, ROWS)
        dgu_t[pl.ds(0, HID), pl.ds(lo, ROWS)] = dgate.T.astype(BF)
        dgu_t[pl.ds(HID, HID), pl.ds(lo, ROWS)] = dup.T.astype(BF)
        hid_t[:, pl.ds(lo, ROWS)] = scaled.T.astype(BF)
        both = jnp.concatenate([dgate, dup], axis=1).astype(BF)
        for s in range(2):
            @pl.loop(0, W // TILE)
            def _(n):
                lo = pl.multiple_of(n * TILE, TILE)
                res = dot_t(both, wgu[pl.ds(s * W + lo, TILE)])
                part[0, s, cc, :, :, :, pl.ds(lo, TILE)] = res.astype(BF).reshape(4, 4, TOK, TILE)

    def grad_tiles(s, first, last):
        @pl.loop(first, last)
        def _(n):
            lo = pl.multiple_of(n * TILE, TILE)
            g = (g0, g1)[s]
            rows = g[ROWS_B, :, :, :, :, pl.ds(lo, TILE)].reshape(2 * ROWS, TILE)
            here = pl.ds(s * W + lo, TILE)
            res = dot(dgu_t[...], rows)
            mg[here] = (mg[here].astype(F32) + res[:HID].T).astype(BF)
            mu[here] = (mu[here].astype(F32) + res[HID:].T).astype(BF)
            cot = g[GRADS, :, :, :, :, pl.ds(lo, TILE)].reshape(2 * ROWS, TILE)
            md[:, here] = (md[:, here].astype(F32) + dot(hid_t[...], cot)).astype(BF)

    gens = {
        "b": (ag(ROWS_B, 1), ag(ROWS_B, 0)),
        "c": (ag(GRADS, 1), ag(GRADS, 0)),
        "f": (ag(FRONT, 1), ag(FRONT, 0)),
        "r": (rs(0, 0), rs(0, 1)),
        "q": (rs(1, 0), rs(1, 1)),
    }
    ins = [
        pltpu.make_async_copy(src, dst, in_sem.at[i])
        for i, (src, dst) in enumerate((
            (saved_in, saved), (gain_in, gain), (ids_b_in, ids_b), (aff_b_in, aff_b),
            (ids_f_in, ids_f), (aff_f_in, aff_f), (turn_in, turn), (fresh_in, fresh),
        ))
    ]
    sec_copies = [
        remote(sent_b, came_b, sec_send.at[0], sec_recv.at[0], dev_s[1]),
        remote(sent_f, came_f, sec_send.at[1], sec_recv.at[1], dev_s[0]),
    ]
    saves = [
        pltpu.make_async_copy(mg, o_gate, save_sem.at[0]),
        pltpu.make_async_copy(mu, o_up, save_sem.at[1]),
        pltpu.make_async_copy(md, o_down, save_sem.at[2]),
    ]

    def start_all(copies):
        for copy in copies:
            copy.start()

    def wait_all(copies):
        for copy in copies:
            copy.wait()

    def enter():
        start_all(ins)
        barrier = pltpu.get_barrier_semaphore()
        for dev in (dev_z, dev_c, *dev_y, *dev_x, *dev_s):
            pl.semaphore_signal(barrier, inc=1, device_id=dev, device_id_type=MESH)
        wait_all(ins[:4])
        place(ROWS_B, norm(saved[...]), weights_of(ids_b, aff_b))
        pl.semaphore_wait(barrier, 8)

    def place_grads():
        wait_all(ins[4:])
        sec_copies[0].wait_recv()
        upstream = jnp.where(sec == 3, turn[...], came_b[...])
        came_b[...] = upstream
        place(GRADS, upstream)

    def place_front():
        sec_copies[1].wait_recv()
        front = jnp.where(sec == 0, fresh[...], came_f[...])
        came_f[...] = front
        place(FRONT, norm(front), weights_of(ids_f, aff_f))

    def finish_back():
        values = saved[...].astype(F32)
        inverse = rinv_of(values)
        scaled = total_of(0) * gain[...].astype(F32)
        mean = jnp.mean(scaled * values, axis=-1, keepdims=True)
        out_b[...] = (
            came_b[...].astype(F32)
            + inverse * scaled
            - inverse * inverse * inverse * values * mean
        ).astype(BF)

    def finish_front():
        out_f[...] = (came_f[...].astype(F32) + total_of(1)).astype(BF)

    work = {
        "enter": enter,
        "sec": lambda: start_all(sec_copies),
        "load": lambda: start_all(loads),
        "C": place_grads,
        "F": place_front,
        "W": lambda: wait_all(loads[:3]),
        "P0": lambda: back_acts(0),
        "P1": lambda: back_acts(1),
        "K0": lambda: back_chunk(0),
        "K1": lambda: back_chunk(1),
        "H0": lambda: front_chunk(0),
        "H1": lambda: front_chunk(1),
        "M": lambda: wait_all(loads[3:]),
        "G0": lambda: grad_tiles(0, 0, 2),
        "G1": lambda: grad_tiles(0, 2, 4),
        "G2": lambda: grad_tiles(0, 4, 7),
        "G3": lambda: grad_tiles(1, 0, 2),
        "G4": lambda: grad_tiles(1, 2, 4),
        "G5": lambda: grad_tiles(1, 4, 7),
        "save": lambda: start_all(saves),
        "ws": lambda: [copy.wait_send() for copy in pending],
        "wr": lambda: [copy.wait_send() for copy in done[:28]],
        "eb": finish_back,
        "ef": finish_front,
    }
    for token in ORDER:
        if token[0] in gens:
            for g in gens[token[0]] if len(token) == 1 else (gens[token[0]][int(token[1])],):
                next(g, None)
        else:
            work[token]()

    for copy in sec_copies:
        copy.wait_send()
    for copy in done[28:]:
        copy.wait_send()
    wait_all(saves)


def hand_over(*refs):
    held, came, went = refs[10:15], refs[15], refs[16]
    order = (2, 3, 4, 0, 1)
    ins = {i: pltpu.make_async_copy(refs[i], held[i], came.at[i]) for i in order}
    outs = {i: pltpu.make_async_copy(held[i], refs[5 + i].at[0], went.at[i]) for i in order}
    for i in order:
        ins[i].start()
    for i in order:
        ins[i].wait()
        outs[i].start()
    for i in order:
        outs[i].wait()


def body(*args):
    (fresh, sent_f, sent_b, turn, saved, gain, ids_f, aff_f, ids_b, aff_b,
     w_gate, w_up, w_down, m_gate, m_up, m_down) = args
    vmem = pl.BlockSpec(memory_space=pltpu.VMEM)
    hbm = pl.BlockSpec(memory_space=pl.ANY)
    sds = jax.ShapeDtypeStruct
    dma = pltpu.SemaphoreType.DMA
    outs = pl.pallas_call(
        kernel,
        out_shape=(
            sds((TOK, D), BF), sds((TOK, D), BF),
            sds((D, HID), BF), sds((D, HID), BF), sds((HID, D), BF),
        ),
        in_specs=[hbm] * 16,
        out_specs=(vmem, vmem, hbm, hbm, hbm),
        scratch_shapes=[
            pltpu.VMEM((2, 3, 4, 2, TOK, W + 128), BF),
            pltpu.VMEM((3, 2, 4, 4, TOK, W + 128), BF),
            pltpu.VMEM((3, 2, 4, 4, TOK, W), BF),
            pltpu.VMEM((3, 3, 4, TOK, W + 128), BF),
            pltpu.VMEM((3, 4, TOK, W), BF),
            pltpu.VMEM((3, 2, 2, TOK, W + 128), BF),
            pltpu.VMEM((2, 2, 2, 4, 4, TOK, W), BF),
            pltpu.VMEM((4, 4, 4, TOK, W), BF),
            pltpu.VMEM((2, 3, 4, TOK, W), BF),
            pltpu.VMEM((2, 2, 2, TOK, W), BF),
            pltpu.VMEM((2, 3, 4, TOK, W), BF),
            pltpu.VMEM((4, 4, 2, TOK, W), BF),
            pltpu.VMEM((4, 2, 3, TOK, W), BF),
            pltpu.VMEM((4, TOK, W), BF),
            pltpu.VMEM((2, 128, 256), BF),
            pltpu.VMEM((2, 128, 128), BF),
            pltpu.VMEM((2, 256, 128), BF),
            pltpu.VMEM((2, 128, 128), BF),
            pltpu.VMEM((D, 2 * HID), BF),
            pltpu.VMEM((HID, D), BF),
            pltpu.VMEM((D, HID), BF),
            pltpu.VMEM((D, HID), BF),
            pltpu.VMEM((HID, D), BF),
            pltpu.VMEM((2 * HID, 2 * ROWS), BF),
            pltpu.VMEM((HID, 2 * ROWS), BF),
            pltpu.VMEM((2, ROWS, 2 * HID), F32),
            pltpu.VMEM((TOK, D), BF),
            pltpu.VMEM((TOK, D), BF),
            pltpu.VMEM((TOK, D), BF),
            pltpu.VMEM((TOK, D), BF),
            pltpu.VMEM((TOK, D), BF),
            pltpu.VMEM((1, D), BF),
            pltpu.VMEM((2, TOK), jnp.int32),
            pltpu.VMEM((2, TOK), F32),
            pltpu.VMEM((2, TOK), jnp.int32),
            pltpu.VMEM((2, TOK), F32),
            dma((6 * N_AG,)), dma((6 * N_AG,)),
            dma((4 * N_RS,)), dma((4 * N_RS,)),
            dma((2,)), dma((2,)), dma((6,)), dma((3,)), dma((8,)),
        ],
        compiler_params=pltpu.CompilerParams(
            collective_id=0, has_side_effects=True, vmem_limit_bytes=60 * 2**20
        ),
    )(
        fresh, sent_f[0], sent_b[0], turn, saved[0], gain, ids_f[0].T, aff_f[0].T, ids_b[0].T, aff_b[0].T,
        w_gate[0], w_up[0], w_down[0], m_gate[0], m_up[0], m_down[0],
    )
    return pl.pallas_call(
        hand_over,
        out_shape=tuple(sds((1, *o.shape), BF) for o in outs),
        in_specs=[hbm] * 5,
        out_specs=(hbm,) * 5,
        scratch_shapes=[*(pltpu.VMEM(o.shape, BF) for o in outs), dma((5,)), dma((5,))],
    )(*outs)


def solution(mesh):
    rows = P("section", "ep", None)
    cols = P("section", None, "ep")
    return jax.shard_map(
        body,
        mesh=mesh,
        in_specs=(
            P("ep", None), rows, rows, P("ep", None), rows, P("section", None),
            rows, rows, rows, rows, cols, cols, rows, cols, cols, rows,
        ),
        out_specs=(rows, rows, cols, cols, rows),
        check_vma=False,
    )
```

```python
import functools
import jax
import jax.numpy as jnp
from jax import lax
from jax.experimental import pallas as pl
from jax.experimental.pallas import tpu as pltpu
from jax.sharding import PartitionSpec as P

BF = jnp.bfloat16
F32 = jnp.float32
MESH = pl.DeviceIdType.MESH
D = 3584
W = D // 2
TOK = 16
HID = 128
EXPERTS = 8
ROWS = 256
TILE = 256
CAP = 8
ROWS_B, GRADS, FRONT = 0, 1, 2
N_AG = 20
ORDER = (
    "enter", "b", "sec", "load", "b", "b", "C", "c", "F", "f", "b", "b", "c", "f", "c", "f",
    "b", "c", "f", "c", "b", "f", "b", "c", "W", "b", "P0", "c", "P1", "c", "c", "f",
    "K0", "f", "r", "K1", "r", "f", "f", "H0", "q", "r", "H1", "q", "r", "r", "q", "r",
    "q", "M", "G0", "r", "q", "G1", "r", "q", "G2", "r", "eb", "G3", "q", "G4", "q", "G5",
    "save", "ws", "wr", "q", "ef",
)
N_RS = 14


def kernel(
    fresh_in, sent_f, sent_b, turn_in, saved_in, gain_in, ids_f_in, aff_f_in, ids_b_in, aff_b_in,
    w_gate, w_up, w_down, m_gate, m_up, m_down,
    out_f, out_b, o_gate, o_up, o_down,
    tk, g0, g1, packed_y, packed_x, relay, part, core_in, slots_y, relay_back, slots_x,
    tokens, small_in, last_in, pick_y, pick_x, pick_y_t, pick_x_t,
    wgu, wd, mg, mu, md, dgu_t, hid_t, acts, wgu_t, wd_t, came_f, came_b,
    fresh, turn, saved, gain, ids_f, aff_f, ids_b, aff_b,
    ag_send, ag_recv, rs_send, rs_recv, sec_send, sec_recv, load_sem, save_sem, in_sem,
):
    sec = lax.axis_index("section")
    ep = lax.axis_index("ep")
    core = lax.rem(ep, 2)
    z = lax.rem(ep // 2, 2)
    x = lax.rem(ep // 4, 4)
    y = ep // 16
    expert = ep // 8
    pair = x // 2
    x_in = x + 1 - 2 * lax.rem(x, 2)

    def at(yy, xx, zz, cc):
        return (sec, ((yy * 4 + xx) * 2 + zz) * 2 + cc)

    def turn4(v, by):
        return lax.rem(v + by, 4)

    dev_z = at(y, x, 1 - z, core)
    dev_c = at(y, x, z, 1 - core)
    dev_y = (at(turn4(y, 1), x, z, core), at(turn4(y, 3), x, z, core))
    dev_x = (at(y, turn4(x, 1), z, core), at(y, turn4(x, 3), z, core))
    x_out = turn4(x, 3 + 2 * lax.rem(x, 2))
    x_far = turn4(x, 2)
    dev_in, dev_out = at(y, x_in, z, core), at(y, x_out, z, core)
    dev_s = ((turn4(sec, 1), ep), (turn4(sec, 3), ep))

    loads = [
        pltpu.make_async_copy(w_gate, wgu.at[:, pl.ds(0, HID)], load_sem.at[0]),
        pltpu.make_async_copy(w_up, wgu.at[:, pl.ds(HID, HID)], load_sem.at[1]),
        pltpu.make_async_copy(w_down, wd, load_sem.at[2]),
        pltpu.make_async_copy(m_gate, mg, load_sem.at[3]),
        pltpu.make_async_copy(m_up, mu, load_sem.at[4]),
        pltpu.make_async_copy(m_down, md, load_sem.at[5]),
    ]

    def remote(src, dst, send, recv, dev):
        return pltpu.make_async_remote_copy(
            src_ref=src, dst_ref=dst, send_sem=send, recv_sem=recv,
            device_id=dev, device_id_type=MESH,
        )

    every = slice(None)
    lane128 = lax.broadcasted_iota(jnp.int32, (128, 128), 1)
    row128 = lax.broadcasted_iota(jnp.int32, (128, 128), 0)
    route_of = (0, 0, 1)
    width_of = (W + 128, W, W + 128)

    def build_picks(u, s):
        route = route_of[u]
        aux = tk[s, u, :, :, :, pl.ds(W, 128)].reshape(128, 128)
        named = jnp.where((aux.astype(F32) > 0.0) & (lane128 < EXPERTS), 1.0, 0.0)
        before = jnp.where((row128 // TOK == lane128 // TOK) & (lane128 < row128), 1.0, 0.0)
        order = dot(before.astype(BF), named.astype(BF))
        block = lax.broadcasted_iota(jnp.int32, (128, 1), 0) // TOK

        def places(e):
            chosen = jnp.sum(jnp.where(lane128 == e, named, 0.0), axis=1, keepdims=True)
            slot = jnp.sum(jnp.where(lane128 == e, order, 0.0), axis=1, keepdims=True)
            return chosen, block * CAP + slot.astype(jnp.int32)

        if s == 0:
            wanted = [2 * turn4(y, r) + pair for r in range(4)]
        else:
            wanted = [2 * y + pair, 2 * y + 1 - pair]
        lane = lax.broadcasted_iota(jnp.int32, (128, 64 * len(wanted)), 1)
        pick = jnp.zeros((128, 64 * len(wanted)), F32)
        for r, e in enumerate(wanted):
            chosen, target = places(e)
            pick = pick + jnp.where(lane == target + 64 * r, chosen, 0.0)
        (pick_y, pick_x)[s][route] = pick.astype(BF)
        (pick_y_t, pick_x_t)[s][route] = pick.T.astype(BF)

    def pack(u, s):
        route = route_of[u]
        if u != GRADS:
            build_picks(u, s)

        def tile(lo, size):
            rows = tk[s, u, :, :, :, pl.ds(lo, size)].reshape(128, size)
            res = dot((pick_y_t, pick_x_t)[s][route], rows).astype(BF)
            if s == 0:
                g0[u, core, y, :, :, pl.ds(lo, size)] = res[:64].reshape(4, TOK, size)
                for r in range(3):
                    packed_y[u, r, :, :, pl.ds(lo, size)] = (
                        res[64 * (r + 1) : 64 * (r + 2)].reshape(4, TOK, size)
                    )
            else:
                g1[u, core, :, x, :, pl.ds(lo, size)] = res[:64].reshape(4, TOK, size)
                packed_x[u, :, :, pl.ds(lo, size)] = res[64:].reshape(4, TOK, size)

        @pl.loop(0, W // TILE)
        def _(n):
            tile(pl.multiple_of(n * TILE, TILE), TILE)

        if s == 0 and u != GRADS:
            tile(W, 128)

    pending = []

    def ag(u, s):
        base = (u * 2 + s) * N_AG

        def put(k, src, dst, dev):
            copy = remote(src, dst, ag_send.at[base + k], ag_recv.at[base + k], dev)
            copy.start()
            pending.append(copy)

        def got(k, ref):
            remote(ref, ref, ag_send.at[base + k], ag_recv.at[base + k], dev_c).wait_recv()

        me, dev = ((x, dev_x), (y, dev_y))[s]

        def blk(i, h):
            return tk.at[s, u, i, h, :, pl.ds(0, width_of[u])]

        def same(k, ref, to):
            put(k, ref, ref, to)

        left, right, far = turn4(me, 3), turn4(me, 1), turn4(me, 2)
        if u == ROWS_B:
            same(0, blk(me, z), dev_z)
            same(1, blk(me, z), dev[0])
            same(3, blk(me, z), dev[1])
            yield
            got(0, blk(me, 1 - z))
            same(2, blk(me, 1 - z), dev[0])
            same(4, blk(me, 1 - z), dev[1])
            yield
            got(1, blk(left, z))
            same(5, blk(left, z), dev[0])
            got(4, blk(right, 1 - z))
            same(6, blk(right, 1 - z), dev[1])
            yield
            got(2, blk(left, 1 - z))
            got(3, blk(right, z))
            yield
            got(5, blk(far, z))
            got(6, blk(far, 1 - z))
        else:
            near = pl.ds(0, W // 2)
            rest = pl.ds(W // 2, width_of[u] - W // 2)

            def some(i, cols):
                return tk.at[s, u, i, z, :, cols]

            same(1, blk(me, z), dev[0])
            same(3, blk(me, z), dev[1])
            same(0, blk(me, z), dev_z)
            yield
            got(1, blk(left, z))
            same(5, some(left, near), dev[0])
            got(3, blk(right, z))
            same(6, some(right, rest), dev[1])
            same(2, blk(left, z), dev_z)
            same(4, blk(right, z), dev_z)
            yield
            got(5, some(far, near))
            got(6, some(far, rest))
            same(17, blk(far, z), dev_z)
            yield
            got(0, blk(me, 1 - z))
            got(2, blk(left, 1 - z))
            got(4, blk(right, 1 - z))
            yield
            got(17, blk(far, 1 - z))
        pack(u, s)
        if s == 0:
            wide = pl.ds(0, width_of[u])

            def home(cc, yy, xx):
                return g0.at[u, cc, yy, xx, :, wide]

            low, high = pl.ds(0, 2), pl.ds(2, 2)
            up, down, over = turn4(y, 1), turn4(y, 3), turn4(y, 2)
            put(7, packed_y.at[u, 1, low, :, wide], relay.at[u, 0, :, :, wide], dev_y[0])
            put(8, packed_y.at[u, 1, high, :, wide], relay.at[u, 1, :, :, wide], dev_y[1])
            put(9, packed_y.at[u, 0, :, :, wide], home(core, y, every), dev_y[0])
            put(10, packed_y.at[u, 2, :, :, wide], home(core, y, every), dev_y[1])
            same(13, home(core, y, every), dev_c)
            yield
            got(7, relay.at[u, 0, :, :, wide])
            put(11, relay.at[u, 0, :, :, wide], home(core, down, low), dev_y[0])
            got(8, relay.at[u, 1, :, :, wide])
            put(12, relay.at[u, 1, :, :, wide], home(core, up, high), dev_y[1])
            yield
            got(9, home(core, down, every))
            same(14, home(core, down, every), dev_c)
            got(10, home(core, up, every))
            same(15, home(core, up, every), dev_c)
            yield
            got(11, home(core, over, low))
            got(12, home(core, over, high))
            same(16, home(core, over, every), dev_c)
            yield
            for k, i in ((13, y), (14, down), (15, up), (16, over)):
                got(k, home(1 - core, i, every))
        else:

            def home(cc, yy, xx):
                return g1.at[u, cc, yy, xx]

            low, high = pl.ds(0, 2), pl.ds(2, 2)
            put(7, packed_x.at[u, low], home(core, low, x), dev_out)
            same(9, home(core, every, x), dev_in)
            put(8, packed_x.at[u, high], home(core, high, x), dev_out)
            same(13, home(core, every, x), dev_c)
            yield
            got(7, home(core, low, x_out))
            same(10, home(core, low, x_out), dev_in)
            yield
            got(8, home(core, high, x_out))
            same(11, home(core, high, x_out), dev_in)
            same(14, home(core, every, x_out), dev_c)
            got(9, home(core, every, x_in))
            same(15, home(core, every, x_in), dev_c)
            yield
            got(10, home(core, low, x_far))
            got(11, home(core, high, x_far))
            same(16, home(core, every, x_far), dev_c)
            yield
            for k, i in ((13, x), (14, x_out), (15, x_in), (16, x_far)):
                got(k, home(1 - core, every, i))

    done = []

    def add_into(dst, *srcs):
        total = dst[...].astype(F32)
        for src in srcs:
            total = total + src[...].astype(F32)
        dst[...] = total.astype(BF)

    def rs(u, s):
        q = u * 2 + s
        base = q * N_RS

        def put(k, src, dst, dev):
            copy = remote(src, dst, rs_send.at[base + k], rs_recv.at[base + k], dev)
            copy.start()
            done.append(copy)

        def got(k, ref):
            remote(ref, ref, rs_send.at[base + k], rs_recv.at[base + k], dev_c).wait_recv()

        put(0, part.at[u, s, 1 - core], core_in.at[q], dev_c)
        yield
        got(0, core_in.at[q])

        @pl.loop(0, 4)
        def _(yy):
            for xx in range(4):
                add_into(part.at[u, s, core, yy, xx], core_in.at[q, yy, xx])

        if s == 0:
            low, high = pl.ds(0, 2), pl.ds(2, 2)
            up, down, over = turn4(y, 1), turn4(y, 3), turn4(y, 2)
            put(1, part.at[u, s, core, over, low], relay_back.at[u, 0], dev_y[0])
            put(2, part.at[u, s, core, over, high], relay_back.at[u, 1], dev_y[1])
            put(3, part.at[u, s, core, up], slots_y.at[u, 2], dev_y[0])
            put(4, part.at[u, s, core, down], slots_y.at[u, 0], dev_y[1])
            yield
            got(1, relay_back.at[u, 0])
            put(5, relay_back.at[u, 0], slots_y.at[u, 1, low], dev_y[0])
            got(2, relay_back.at[u, 1])
            put(6, relay_back.at[u, 1], slots_y.at[u, 1, high], dev_y[1])
            yield
            got(3, slots_y.at[u, 2])
            got(4, slots_y.at[u, 0])
            yield
            got(5, slots_y.at[u, 1, low])
            got(6, slots_y.at[u, 1, high])
        else:
            low, high = pl.ds(0, 2), pl.ds(2, 2)
            put(1, part.at[u, s, core, low, x_far], slots_x.at[u, 0, low], dev_in)
            put(4, part.at[u, s, core, high, x_far], slots_x.at[u, 0, high], dev_in)
            put(2, part.at[u, s, core, :, x_in], slots_x.at[u, 1], dev_in)
            yield
            for k, out, half in ((1, 3, low), (4, 5, high)):
                got(k, slots_x.at[u, 0, half])
                add_each(part.at[u, s, core, half, x_out], slots_x.at[u, 0, half], 2)
                put(out, part.at[u, s, core, half, x_out], slots_x.at[u, 2, half], dev_out)
            yield
            got(2, slots_x.at[u, 1])
            add_each(part.at[u, s, core, :, x], slots_x.at[u, 1], 4)
            yield
            got(3, slots_x.at[u, 2, low])
            got(5, slots_x.at[u, 2, high])

        @pl.loop(0, W // TILE)
        def _(n):
            here = pl.ds(pl.multiple_of(n * TILE, TILE), TILE)
            if s == 0:
                pick = pick_y[u]
                rows = [part[u, s, core, y, :, :, here].reshape(64, TILE)] + [
                    slots_y[u, r, :, :, here].reshape(64, TILE) for r in range(3)
                ]
            else:
                pick = pick_x[u]
                rows = [
                    part[u, s, core, :, x, :, here].reshape(64, TILE),
                    slots_x[u, 2, :, :, here].reshape(64, TILE),
                ]
            res = dot(pick, jnp.concatenate(rows, axis=0)).astype(BF)
            tokens[q, :, :, :, here] = res.reshape(4, 2, TOK, TILE)

        me, dev = ((x, dev_x), (y, dev_y))[s]
        left, right, far = turn4(me, 3), turn4(me, 1), turn4(me, 2)

        def blk(i, h):
            return tokens.at[q, i, h]

        def buf(d, j):
            return small_in.at[q, d, j]

        put(7, blk(far, 0), buf(0, 0), dev[0])
        put(8, blk(far, 1), buf(1, 0), dev[1])
        put(9, blk(right, 1), buf(0, 2), dev[0])
        put(10, blk(left, 0), buf(1, 1), dev[1])
        yield
        got(7, buf(0, 0))
        add_into(blk(right, 0), buf(0, 0))
        put(11, blk(right, 0), buf(0, 1), dev[0])
        got(8, buf(1, 0))
        add_into(blk(left, 1), buf(1, 0))
        put(12, blk(left, 1), buf(1, 2), dev[1])
        yield
        got(9, buf(0, 2))
        got(10, buf(1, 1))
        yield
        got(11, buf(0, 1))
        got(12, buf(1, 2))
        add_into(blk(me, 0), buf(0, 1), buf(1, 1))
        add_into(blk(me, 1), buf(0, 2), buf(1, 2))
        put(13, blk(me, 1 - z), last_in.at[q], dev_z)
        yield
        got(13, last_in.at[q])

    def add_each(dst, src, count):
        for i in range(count):
            add_into(dst.at[i], src.at[i])

    def total_of(u):
        halves = [
            tokens[u * 2 + s, (x, y)[s], z].astype(F32) + last_in[u * 2 + s].astype(F32)
            for s in range(2)
        ]
        return jnp.concatenate(halves, axis=1)

    def rinv_of(v):
        return lax.rsqrt(jnp.mean(v * v, axis=-1, keepdims=True) + 1e-6)

    def place(u, value, weights=None):
        tk[0, u, x, z, :, pl.ds(0, W)] = value[:, :W]
        tk[1, u, y, z, :, pl.ds(0, W)] = value[:, W:]
        if weights is not None:
            tk[0, u, x, z, :, pl.ds(W, 128)] = weights
            tk[1, u, y, z, :, pl.ds(W, 128)] = weights

    def norm(ref):
        v = ref.astype(F32)
        return (v * rinv_of(v) * gain[...].astype(F32)).astype(BF)

    def weights_of(ids, aff):
        lane = lax.broadcasted_iota(jnp.int32, (TOK, 128), 1)
        eye = lax.broadcasted_iota(jnp.int32, (TOK, TOK), 0) == lax.broadcasted_iota(
            jnp.int32, (TOK, TOK), 1
        )

        def column(row):
            wide = jnp.broadcast_to(row.astype(F32), (TOK, TOK))
            return jnp.sum(jnp.where(eye, wide, 0.0), axis=1, keepdims=True)

        named = [column(ids[k : k + 1, :]).astype(jnp.int32) for k in range(2)]
        both = [column(aff[k : k + 1, :]) for k in range(2)]
        out = jnp.zeros((TOK, 128), F32)
        for k in range(2):
            one = both[k] / (both[0] + both[1])
            high = one.astype(BF).astype(F32)
            out = out + jnp.where(lane == named[k], high, 0.0)
            out = out + jnp.where(lane == named[k] + EXPERTS, one - high, 0.0)
        return out.astype(BF)

    def rows_of(u, cc):
        a = g0[u, cc, :, :, :, pl.ds(0, W)].reshape(ROWS, W)
        b = g1[u, cc].reshape(ROWS, W)
        return a, b

    def share_of(u, cc):
        aux = g0[u, cc, :, :, :, pl.ds(W, 128)].reshape(ROWS, 128).astype(F32)
        lane = lax.broadcasted_iota(jnp.int32, (ROWS, 128), 1)
        mine = (lane == expert) | (lane == expert + EXPERTS)
        return jnp.sum(jnp.where(mine, aux, 0.0), axis=1, keepdims=True)

    def dot(a, b):
        return jnp.dot(a, b, preferred_element_type=F32)

    def turn_weights():
        wait_all(loads[:3])

        @pl.loop(0, D // TILE)
        def _(n):
            here = pl.ds(pl.multiple_of(n * TILE, TILE), TILE)
            wgu_t[:, here] = wgu[here].astype(F32).T.astype(BF)
            wd_t[here] = wd[:, here].astype(F32).T.astype(BF)

    def pre_acts(u, cc):
        a, b = rows_of(u, cc)
        return dot(a, wgu[pl.ds(0, W)]) + dot(b, wgu[pl.ds(W, W)])

    def back_acts(i):
        acts[i] = pre_acts(ROWS_B, (1 - core, core)[i])

    def front_chunk(i):
        cc = (1 - core, core)[i]
        both = pre_acts(FRONT, cc)
        gate, up = both[:, :HID], both[:, HID:]
        hidden = (gate * jax.nn.sigmoid(gate) * up * share_of(FRONT, cc)).astype(BF)
        for s in range(2):
            @pl.loop(0, W // TILE)
            def _(n):
                lo = pl.multiple_of(n * TILE, TILE)
                res = dot(hidden, wd[:, pl.ds(s * W + lo, TILE)])
                part[1, s, cc, :, :, :, pl.ds(lo, TILE)] = res.astype(BF).reshape(4, 4, TOK, TILE)

    def back_chunk(i):
        cc = (1 - core, core)[i]
        gate, up = acts[i, :, :HID], acts[i, :, HID:]
        a, b = rows_of(GRADS, cc)
        share = share_of(ROWS_B, cc)
        sig = jax.nn.sigmoid(gate)
        active = gate * sig
        grad_hidden = (dot(a, wd_t[pl.ds(0, W)]) + dot(b, wd_t[pl.ds(W, W)])) * share
        dgate = grad_hidden * up * sig * (1.0 + gate * (1.0 - sig))
        dup = grad_hidden * active
        scaled = active * up * share
        lo = pl.multiple_of(cc * ROWS, ROWS)
        dgu_t[pl.ds(0, HID), pl.ds(lo, ROWS)] = dgate.T.astype(BF)
        dgu_t[pl.ds(HID, HID), pl.ds(lo, ROWS)] = dup.T.astype(BF)
        hid_t[:, pl.ds(lo, ROWS)] = scaled.T.astype(BF)
        both = jnp.concatenate([dgate, dup], axis=1).astype(BF)
        for s in range(2):
            @pl.loop(0, W // TILE)
            def _(n):
                lo = pl.multiple_of(n * TILE, TILE)
                res = dot(both, wgu_t[:, pl.ds(s * W + lo, TILE)])
                part[0, s, cc, :, :, :, pl.ds(lo, TILE)] = res.astype(BF).reshape(4, 4, TOK, TILE)

    def grad_tiles(s, first, last):
        @pl.loop(first, last)
        def _(n):
            lo = pl.multiple_of(n * TILE, TILE)
            g = (g0, g1)[s]
            rows = g[ROWS_B, :, :, :, :, pl.ds(lo, TILE)].reshape(2 * ROWS, TILE)
            here = pl.ds(s * W + lo, TILE)
            res = dot(dgu_t[...], rows)
            mg[here] = (mg[here].astype(F32) + res[:HID].T).astype(BF)
            mu[here] = (mu[here].astype(F32) + res[HID:].T).astype(BF)
            cot = g[GRADS, :, :, :, :, pl.ds(lo, TILE)].reshape(2 * ROWS, TILE)
            md[:, here] = (md[:, here].astype(F32) + dot(hid_t[...], cot)).astype(BF)

    gens = {
        "b": (ag(ROWS_B, 1), ag(ROWS_B, 0)),
        "c": (ag(GRADS, 1), ag(GRADS, 0)),
        "f": (ag(FRONT, 1), ag(FRONT, 0)),
        "r": (rs(0, 0), rs(0, 1)),
        "q": (rs(1, 0), rs(1, 1)),
    }
    ins = [
        pltpu.make_async_copy(src, dst, in_sem.at[i])
        for i, (src, dst) in enumerate((
            (saved_in, saved), (gain_in, gain), (ids_b_in, ids_b), (aff_b_in, aff_b),
            (ids_f_in, ids_f), (aff_f_in, aff_f), (turn_in, turn), (fresh_in, fresh),
        ))
    ]
    sec_copies = [
        remote(sent_b, came_b, sec_send.at[0], sec_recv.at[0], dev_s[1]),
        remote(sent_f, came_f, sec_send.at[1], sec_recv.at[1], dev_s[0]),
    ]
    saves = [
        pltpu.make_async_copy(mg, o_gate, save_sem.at[0]),
        pltpu.make_async_copy(mu, o_up, save_sem.at[1]),
        pltpu.make_async_copy(md, o_down, save_sem.at[2]),
    ]

    def start_all(copies):
        for copy in copies:
            copy.start()

    def wait_all(copies):
        for copy in copies:
            copy.wait()

    def enter():
        start_all(ins)
        barrier = pltpu.get_barrier_semaphore()
        for dev in (dev_z, dev_c, *dev_y, *dev_x, *dev_s):
            pl.semaphore_signal(barrier, inc=1, device_id=dev, device_id_type=MESH)
        wait_all(ins[:4])
        place(ROWS_B, norm(saved[...]), weights_of(ids_b, aff_b))
        pl.semaphore_wait(barrier, 8)

    def place_grads():
        wait_all(ins[4:])
        sec_copies[0].wait_recv()
        upstream = jnp.where(sec == 3, turn[...], came_b[...])
        came_b[...] = upstream
        place(GRADS, upstream)

    def place_front():
        sec_copies[1].wait_recv()
        front = jnp.where(sec == 0, fresh[...], came_f[...])
        came_f[...] = front
        place(FRONT, norm(front), weights_of(ids_f, aff_f))

    def finish_back():
        values = saved[...].astype(F32)
        inverse = rinv_of(values)
        scaled = total_of(0) * gain[...].astype(F32)
        mean = jnp.mean(scaled * values, axis=-1, keepdims=True)
        out_b[...] = (
            came_b[...].astype(F32)
            + inverse * scaled
            - inverse * inverse * inverse * values * mean
        ).astype(BF)

    def finish_front():
        out_f[...] = (came_f[...].astype(F32) + total_of(1)).astype(BF)

    work = {
        "enter": enter,
        "sec": lambda: start_all(sec_copies),
        "load": lambda: start_all(loads),
        "C": place_grads,
        "F": place_front,
        "W": turn_weights,
        "P0": lambda: back_acts(0),
        "P1": lambda: back_acts(1),
        "K0": lambda: back_chunk(0),
        "K1": lambda: back_chunk(1),
        "H0": lambda: front_chunk(0),
        "H1": lambda: front_chunk(1),
        "M": lambda: wait_all(loads[3:]),
        "G0": lambda: grad_tiles(0, 0, 2),
        "G1": lambda: grad_tiles(0, 2, 4),
        "G2": lambda: grad_tiles(0, 4, 7),
        "G3": lambda: grad_tiles(1, 0, 2),
        "G4": lambda: grad_tiles(1, 2, 4),
        "G5": lambda: grad_tiles(1, 4, 7),
        "save": lambda: start_all(saves),
        "ws": lambda: [copy.wait_send() for copy in pending],
        "wr": lambda: [copy.wait_send() for copy in done[:28]],
        "eb": finish_back,
        "ef": finish_front,
    }
    for token in ORDER:
        if token[0] in gens:
            for g in gens[token[0]] if len(token) == 1 else (gens[token[0]][int(token[1])],):
                next(g, None)
        else:
            work[token]()

    for copy in sec_copies:
        copy.wait_send()
    for copy in done[28:]:
        copy.wait_send()
    wait_all(saves)


def hand_over(*refs):
    held, came, went = refs[10:15], refs[15], refs[16]
    order = (2, 3, 4, 0, 1)
    ins = {i: pltpu.make_async_copy(refs[i], held[i], came.at[i]) for i in order}
    outs = {i: pltpu.make_async_copy(held[i], refs[5 + i].at[0], went.at[i]) for i in order}
    for i in order:
        ins[i].start()
    for i in order:
        ins[i].wait()
        outs[i].start()
    for i in order:
        outs[i].wait()


def body(*args):
    (fresh, sent_f, sent_b, turn, saved, gain, ids_f, aff_f, ids_b, aff_b,
     w_gate, w_up, w_down, m_gate, m_up, m_down) = args
    vmem = pl.BlockSpec(memory_space=pltpu.VMEM)
    hbm = pl.BlockSpec(memory_space=pl.ANY)
    sds = jax.ShapeDtypeStruct
    dma = pltpu.SemaphoreType.DMA
    outs = pl.pallas_call(
        kernel,
        out_shape=(
            sds((TOK, D), BF), sds((TOK, D), BF),
            sds((D, HID), BF), sds((D, HID), BF), sds((HID, D), BF),
        ),
        in_specs=[hbm] * 16,
        out_specs=(vmem, vmem, hbm, hbm, hbm),
        scratch_shapes=[
            pltpu.VMEM((2, 3, 4, 2, TOK, W + 128), BF),
            pltpu.VMEM((3, 2, 4, 4, TOK, W + 128), BF),
            pltpu.VMEM((3, 2, 4, 4, TOK, W), BF),
            pltpu.VMEM((3, 3, 4, TOK, W + 128), BF),
            pltpu.VMEM((3, 4, TOK, W), BF),
            pltpu.VMEM((3, 2, 2, TOK, W + 128), BF),
            pltpu.VMEM((2, 2, 2, 4, 4, TOK, W), BF),
            pltpu.VMEM((4, 4, 4, TOK, W), BF),
            pltpu.VMEM((2, 3, 4, TOK, W), BF),
            pltpu.VMEM((2, 2, 2, TOK, W), BF),
            pltpu.VMEM((2, 3, 4, TOK, W), BF),
            pltpu.VMEM((4, 4, 2, TOK, W), BF),
            pltpu.VMEM((4, 2, 3, TOK, W), BF),
            pltpu.VMEM((4, TOK, W), BF),
            pltpu.VMEM((2, 128, 256), BF),
            pltpu.VMEM((2, 128, 128), BF),
            pltpu.VMEM((2, 256, 128), BF),
            pltpu.VMEM((2, 128, 128), BF),
            pltpu.VMEM((D, 2 * HID), BF),
            pltpu.VMEM((HID, D), BF),
            pltpu.VMEM((D, HID), BF),
            pltpu.VMEM((D, HID), BF),
            pltpu.VMEM((HID, D), BF),
            pltpu.VMEM((2 * HID, 2 * ROWS), BF),
            pltpu.VMEM((HID, 2 * ROWS), BF),
            pltpu.VMEM((2, ROWS, 2 * HID), F32),
            pltpu.VMEM((2 * HID, D), BF),
            pltpu.VMEM((D, HID), BF),
            pltpu.VMEM((TOK, D), BF),
            pltpu.VMEM((TOK, D), BF),
            pltpu.VMEM((TOK, D), BF),
            pltpu.VMEM((TOK, D), BF),
            pltpu.VMEM((TOK, D), BF),
            pltpu.VMEM((1, D), BF),
            pltpu.VMEM((2, TOK), jnp.int32),
            pltpu.VMEM((2, TOK), F32),
            pltpu.VMEM((2, TOK), jnp.int32),
            pltpu.VMEM((2, TOK), F32),
            dma((6 * N_AG,)), dma((6 * N_AG,)),
            dma((4 * N_RS,)), dma((4 * N_RS,)),
            dma((2,)), dma((2,)), dma((6,)), dma((3,)), dma((8,)),
        ],
        compiler_params=pltpu.CompilerParams(
            collective_id=0, has_side_effects=True, vmem_limit_bytes=60 * 2**20
        ),
    )(
        fresh, sent_f[0], sent_b[0], turn, saved[0], gain, ids_f[0].T, aff_f[0].T, ids_b[0].T, aff_b[0].T,
        w_gate[0], w_up[0], w_down[0], m_gate[0], m_up[0], m_down[0],
    )
    return pl.pallas_call(
        hand_over,
        out_shape=tuple(sds((1, *o.shape), BF) for o in outs),
        in_specs=[hbm] * 5,
        out_specs=(hbm,) * 5,
        scratch_shapes=[*(pltpu.VMEM(o.shape, BF) for o in outs), dma((5,)), dma((5,))],
    )(*outs)


def solution(mesh):
    rows = P("section", "ep", None)
    cols = P("section", None, "ep")
    return jax.shard_map(
        body,
        mesh=mesh,
        in_specs=(
            P("ep", None), rows, rows, P("ep", None), rows, P("section", None),
            rows, rows, rows, rows, cols, cols, rows, cols, cols, rows,
        ),
        out_specs=(rows, rows, cols, cols, rows),
        check_vma=False,
    )
```
